32 devices in a mesh: shard: 4 (over z), ctx: 2 (over core), tp: 4 (over y, x).
Axes of the slice: x: 2, y: 2, z: 4, core: 2. Of those that a mesh axis runs over, the one named last changes fastest.
Arguments:
- tokens: bfloat16 [8, 1024, 768], P('shard', 'ctx'), may hold values from -6 to 6
- time_embed: float32 [8, 768], P('shard'), may hold values from -3 to 3
- segments: int32 [8, 1024], P('shard'), may hold values from 0 to 3, never falling along the last dimension, each value on 1 to 800 neighbouring positions
- w_qkv: bfloat16 [768, 3, 768], P('shard', None, 'tp'), may hold values from -0.21875 to 0.21875
- w_out: bfloat16 [768, 768], P('tp', 'shard'), may hold values from -0.875 to 0.875
- w_up: bfloat16 [768, 3072], P('shard', 'tp'), may hold values from -0.21875 to 0.21875
- w_down: bfloat16 [3072, 768], P('tp', 'shard'), may hold values from -0.21875 to 0.21875
- qv_bias: float32 [2, 768], P(None, 'tp'), may hold values from -0.625 to 0.625
- up_bias: float32 [3072], P('tp'), may hold values from -1.75 to 1.75
- norm_gains: float32 [2, 768], replicated, may hold values from 0.5 to 1.5
- norm_shifts: float32 [2, 768], replicated, may hold values from -1.75 to 1.75
- branch_bias: float32 [2, 768], replicated, may hold values from -1.75 to 1.75
- out_grad: bfloat16 [8, 1024, 768], P('shard', 'ctx'), may hold values from -8 to 8
Outputs:
- layer_out: float32 [8, 1024, 768], P('shard', 'ctx')
- input_grad: float32 [8, 1024, 768], P('shard', 'ctx')
- w_qkv_grad: float32 [768, 3, 768], P('shard', None, 'tp')
- w_out_grad: float32 [768, 768], P('tp', 'shard')
- w_up_grad: float32 [768, 3072], P('shard', 'tp')
- w_down_grad: float32 [3072, 768], P('tp', 'shard')
- qv_bias_grad: float32 [2, 768], P(None, 'tp')
- up_bias_grad: float32 [3072], P('tp')
- norm_gains_grad: float32 [2, 768], replicated
- norm_shifts_grad: float32 [2, 768], replicated
- branch_bias_grad: float32 [2, 768], replicated
The draws below stay inside these ranges and needn't reach their ends.
Inputs may be any that keep to these rules, and one draw needn't show every extreme that they name: `segments`: document numbers never fall along a sequence; each document holds 1 to 800 tokens, and one of each sequence exactly 800.
All inputs are finite; a program needn't handle non-finite values.
Results may differ from the reference program's by a relative error of at most 0.018.
Values may be sent and summed in bfloat16 or wider, within the bound.
No kernel may reach another device: no remote copies, remote signals or barrier semaphores. Data moves between devices by JAX's collectives and lax.ppermute only.
A program may use at most 128 MiB of HBM per device.

```python
import math
import jax
import jax.numpy as jnp
import numpy as np
from jax import lax

D = 768
HEADS = 12
HD = 64
FF = 3072
LEN = 1024
DOCS = 4
SEQ_SH = 2
MOST = 800
SEQS = 8


def raised(values, stream_key, source, target, shards_of, factor):
    def block_of(position):
        return (jnp.arange(values.shape[position]) // (values.shape[position] // shards_of)).reshape((-1,) + (1,) * (values.ndim - 1 - position))

    one_side = jax.random.permutation(stream_key, shards_of)[block_of(target)]
    other_side = (block_of(target) + shards_of // 2) % shards_of
    return jnp.where((block_of(source) == one_side) | (block_of(source) == other_side), factor * values, values)


def block_levels(rng, extent, split, smallest, top_value):
    def one(axis_at, blocks):
        draws = jax.random.uniform(jax.random.fold_in(jax.random.fold_in(rng, 6), axis_at), (blocks,), jnp.float32, smallest / len(split), top_value / len(split))
        return jnp.repeat(jnp.exp(draws), extent[axis_at] // blocks).reshape((-1,) + (1,) * (len(extent) - axis_at - 1))

    level = one(*split[0])
    for cut in split[1:]:
        level = level * one(*cut)
    return level


def length_profile(number_of, total, bound, slope):
    portions = [(1 << 20) // math.isqrt(grade ** slope) + 1 for grade in range(2, number_of + 1)]
    spare, holding = total - bound - (number_of - 1), [1] * (number_of - 1)
    while spare > 0:
        free = [i for i in range(number_of - 1) if holding[i] < bound]
        mass, budget = sum([portions[i] for i in free]), spare
        for i in free:
            addition = min(bound - holding[i], max(1, budget * portions[i] // mass), spare)
            holding[i] = holding[i] + addition
            spare = spare - addition
    return np.array([bound] + holding)


def uneven_parts(rng, count, total, bound, slope):
    if count == 2:
        one = jax.random.randint(rng, (), max(1, total - bound), min(bound, total - 1) + 1)
        return jnp.stack([one, total - one])
    tallies = jnp.asarray(length_profile(count, total, bound, slope), jnp.int32)
    twos = (count - 1) // 2
    giver, sink = tallies[1:1 + 2 * twos:2], tallies[2:2 + 2 * twos:2]
    slack = jnp.minimum(giver - 1, bound - sink)
    passed = jax.random.randint(jax.random.fold_in(rng, 1), (twos,), 0, 1 << 20) % (slack + 1)
    tallies = tallies.at[1:1 + 2 * twos:2].set(giver - passed).at[2:2 + 2 * twos:2].set(sink + passed)
    return tallies[jax.random.permutation(jax.random.fold_in(rng, 2), count)]


def bell_draw(stream_key, shape, width, most, cuts=(), dtype=jnp.bfloat16):
    array = width * jax.random.normal(stream_key, shape, jnp.float32)
    if cuts:
        array = array * block_levels(stream_key, shape, cuts, -0.22, 0.18)
    return jnp.clip(array, -most, most).astype(dtype)


def heavy_noise(own_key, shape, deviation, limit, cuts, heavy, held_as=jnp.bfloat16):
    values = deviation * jax.random.normal(own_key, shape, jnp.float32)
    if cuts:
        values = values * block_levels(own_key, shape, cuts, -0.22, 0.18)
    return jnp.clip(raised(values, jax.random.fold_in(own_key, 3), *heavy), -limit, limit).astype(held_as)


def setup_inputs(seed: int = 0) -> dict:
    arg_keys = jax.random.split(jax.random.key(seed), 14)
    return {
        "tokens": bell_draw(arg_keys[0], (SEQS, LEN, D), 1.0, 6.0, ((0, 4), (1, 2))),
        "time_embed": bell_draw(arg_keys[1], (SEQS, D), 0.5, 3.0, ((0, 4),), jnp.float32),
        "segments": jax.vmap(lambda own: jnp.searchsorted(jnp.cumsum(uneven_parts(own, DOCS, LEN, MOST, 1)), jnp.arange(LEN), side="right"))(jax.random.split(arg_keys[2], SEQS)).reshape((SEQS, LEN)).astype(jnp.int32),
        "w_qkv": bell_draw(arg_keys[3], (D, 3, D), D ** -0.5, 0.21875, ((0, 4), (2, 4))),
        "w_out": bell_draw(arg_keys[4], (D, D), (D // 16) ** -0.5, 0.875, ((0, 4), (1, 4))),
        "w_up": bell_draw(arg_keys[5], (D, FF), D ** -0.5, 0.21875, ((0, 4), (1, 4))),
        "w_down": bell_draw(arg_keys[6], (FF, D), (FF // 4) ** -0.5, 0.21875, ((0, 4), (1, 4))),
        "qv_bias": bell_draw(arg_keys[7], (2, D), 0.1, 0.625, ((1, 4),), jnp.float32),
        "up_bias": bell_draw(arg_keys[8], (FF,), 0.3, 1.75, ((0, 4),), jnp.float32),
        "norm_gains": jnp.clip(1.0 + 0.1 * jax.random.normal(arg_keys[9], (2, D), jnp.float32), 0.5, 1.5),
        "norm_shifts": bell_draw(arg_keys[10], (2, D), 0.3, 1.75, (), jnp.float32),
        "branch_bias": bell_draw(arg_keys[11], (2, D), 0.3, 1.75, (), jnp.float32),
        "out_grad": heavy_noise(arg_keys[12], (SEQS, LEN, D), 1.0, 8.0, ((0, 4), (1, 2)), (0, 2, 4, 2.0)),
    }


@jax.custom_vjp
def low(v):
    return lax.optimization_barrier(v.astype(jnp.bfloat16)).astype(jnp.float32)

@jax.custom_vjp
def low_back(v):
    return v

def low_keep(v):
    return (low(v), None)

def low_pass(kept, grad):
    return (grad,)

def back_keep(v):
    return (v, None)

def back_low(kept, grad):
    return (low(grad),)
low.defvjp(low_keep, low_pass)
low_back.defvjp(back_keep, back_low)
highest = lax.Precision.HIGHEST

def layer_norm(residual, gain_vec, shift_vec):
    center = residual - lax.optimization_barrier(jnp.mean(residual, axis=-1, keepdims=True))
    spread = lax.optimization_barrier(jnp.mean(center * center, axis=-1, keepdims=True))
    return center * lax.rsqrt(spread + 1e-05) * gain_vec + shift_vec

def attend(packed):
    query_in, key_in, value_in, labels = packed
    seq_len = query_in.shape[0]
    query_heads = query_in.reshape(seq_len, HEADS, HD)
    key_heads = key_in.reshape(seq_len, HEADS, HD)
    value_heads = value_in.reshape(seq_len, HEADS, HD)
    scores = jnp.einsum('qhe,khe->hqk', query_heads, key_heads, precision=highest) * HD ** (-0.5)
    scores = low_back(scores)
    same_doc = labels[:, None] == labels[None, :]
    scores = jnp.where(same_doc[None], scores, -1e+30)
    attn_probs = jax.nn.softmax(scores, axis=-1)
    heads_out = jnp.einsum('hqk,khe->qhe', low(attn_probs), value_heads, precision=highest)
    return heads_out.reshape(seq_len, D)

def block_forward(tokens_f, w_qkv, w_out, w_up, w_down, qv_bias, up_bias, norm_gains, norm_shifts, branch_bias, time_embed, segments):
    stream_in = tokens_f + time_embed[:, None, :]
    stream_low = low(stream_in)
    product = low_back(jnp.einsum('gld,dcf->glcf', stream_low, w_qkv, precision=highest))
    query_low = low(product[:, :, 0] + qv_bias[0])
    key_low = low(product[:, :, 1])
    value_low = low(product[:, :, 2] + qv_bias[1])
    heads_out = lax.map(jax.checkpoint(attend), (query_low, key_low, value_low, segments))
    heads_low = low(low_back(heads_out))
    attn_out = low_back(jnp.einsum('gld,de->gle', heads_low, w_out, precision=highest)) + branch_bias[0]
    normed = layer_norm(stream_in + attn_out, norm_gains[0], norm_shifts[0])
    pre_act = low_back(jnp.einsum('gld,df->glf', low(normed), w_up, precision=highest)) + up_bias
    act_low = low(jax.nn.gelu(pre_act, approximate=False))
    ffn_out = low_back(jnp.einsum('glf,fd->gld', act_low, w_down, precision=highest)) + branch_bias[1]
    return layer_norm(normed + ffn_out, norm_gains[1], norm_shifts[1])

def reference(tokens, time_embed, segments, w_qkv, w_out, w_up, w_down, qv_bias, up_bias, norm_gains, norm_shifts, branch_bias, out_grad):
    params = tuple((weight_arg.astype(jnp.float32) for weight_arg in (w_qkv, w_out, w_up, w_down, qv_bias, up_bias, norm_gains, norm_shifts, branch_bias)))
    groups = SEQS // SEQ_SH
    inputs = tokens.astype(jnp.float32).reshape(groups, SEQ_SH, LEN, D)
    embeds = time_embed.astype(jnp.float32).reshape(groups, SEQ_SH, D)
    labels_all = segments.astype(jnp.int32).reshape(groups, SEQ_SH, LEN)
    cotangents = out_grad.astype(jnp.float32).reshape(groups, SEQ_SH, LEN, D)

    def group_step(totals, item):
        batch_in, embedding, labels, cotangent = item

        def forward(inputs_f, *weights):
            return block_forward(inputs_f, *weights, embedding, labels)
        result, pullback = jax.vjp(forward, batch_in, *params)
        gradients = pullback(cotangent)
        summed = tuple((total + grad_part for total, grad_part in zip(totals, gradients[1:])))
        return (summed, (result, gradients[0]))
    starts = tuple((jnp.zeros_like(weight_arg) for weight_arg in params))
    totals, (outputs, input_grads) = lax.scan(group_step, starts, (inputs, embeds, labels_all, cotangents))
    return (outputs.reshape(SEQS, LEN, D), input_grads.reshape(SEQS, LEN, D), totals[0], totals[1], totals[2], totals[3], totals[4], totals[5], totals[6], totals[7], totals[8])
```

```python
import math

import jax
import jax.numpy as jnp
from jax import lax
from jax.sharding import PartitionSpec as P

HD = 64
BF = jnp.bfloat16
F32 = jnp.float32


def dot(lhs, rhs, lhs_dim, rhs_dim):
    return lax.dot_general(
        lhs, rhs, (((lhs_dim,), (rhs_dim,)), ((), ())), preferred_element_type=F32
    )


def swap(values, axis, mask):
    size = lax.axis_size(axis)
    return lax.ppermute(values, axis, [(i, i ^ mask) for i in range(size)])


def exchange(chunks, axis):
    return lax.all_to_all(chunks, axis, 0, 0, tiled=True)


def spread(block, axis):
    return exchange(jnp.broadcast_to(block[None], (lax.axis_size(axis), *block.shape)), axis)


def in_order(own, other, index, dim):
    first = jnp.where(index == 0, own, other)
    second = jnp.where(index == 0, other, own)
    return jnp.concatenate([first, second], dim)


def norm_stats(residual):
    center = residual - jnp.mean(residual, axis=-1, keepdims=True)
    spread_of = jnp.mean(center * center, axis=-1, keepdims=True)
    scale = lax.rsqrt(spread_of + 1e-05)
    return center * scale, scale


def norm_grad(scaled, scale, grad, gain_vec):
    weighted = grad * gain_vec
    return scale * (
        weighted
        - jnp.mean(weighted, axis=-1, keepdims=True)
        - scaled * jnp.mean(weighted * scaled, axis=-1, keepdims=True)
    )


def masked_scores(query_blk, key_blk, labels_query, labels_key):
    scores = jnp.einsum("sqhe,skhe->shqk", query_blk, key_blk, preferred_element_type=F32) * HD ** (
        -0.5
    )
    same_doc = labels_query[:, None, :, None] == labels_key[:, None, None, :]
    return jnp.where(same_doc, scores, -1e30)


def attend_forward(query_blk, key_blk, value_blk, labels_query, labels_key):
    scores = masked_scores(query_blk, key_blk, labels_query, labels_key)
    row_max = jnp.max(scores, axis=-1, keepdims=True)
    exp_scores = jnp.exp(scores - row_max)
    row_total = jnp.sum(exp_scores, axis=-1, keepdims=True)
    attn_probs = exp_scores / row_total
    heads_out = jnp.einsum(
        "shqk,skhe->sqhe", attn_probs.astype(BF), value_blk, preferred_element_type=F32
    )
    return heads_out, row_max + jnp.log(row_total)


def attend_backward(query_blk, key_blk, value_blk, labels_query, labels_key, grad_blk, log_total):
    scores = masked_scores(query_blk, key_blk, labels_query, labels_key)
    attn_probs = jnp.exp(scores - log_total)
    grad_probs = jnp.einsum("sqhe,skhe->shqk", grad_blk, value_blk, preferred_element_type=F32)
    inner_sum = jnp.sum(attn_probs * grad_probs, axis=-1, keepdims=True)
    grad_scores = (attn_probs * (grad_probs - inner_sum)).astype(BF)
    grad_query = jnp.einsum(
        "shqk,skhe->sqhe", grad_scores, key_blk, preferred_element_type=F32
    ) * HD ** (-0.5)
    grad_key = jnp.einsum(
        "shqk,sqhe->skhe", grad_scores, query_blk, preferred_element_type=F32
    ) * HD ** (-0.5)
    grad_value = jnp.einsum(
        "shqk,sqhe->skhe", attn_probs.astype(BF), grad_blk, preferred_element_type=F32
    )
    return grad_query, grad_key, grad_value


def shards(
    tokens,
    time_embed,
    segments,
    w_qkv,
    w_out,
    w_up,
    w_down,
    qv_bias,
    up_bias,
    norm_gains,
    norm_shifts,
    branch_bias,
    out_grad,
):
    seqs, half_len, width = tokens.shape
    parts = lax.axis_size("tp")
    deep = lax.axis_size("shard")
    core = lax.axis_index("ctx")
    place = lax.axis_index("tp")
    rows = seqs * half_len
    blk = half_len // parts
    own_rows = seqs * blk
    cols = w_qkv.shape[2]
    heads = cols // HD
    units = w_up.shape[1]
    half_units = units // 2
    depth = w_qkv.shape[0]
    half_depth = depth // 2
    half_cols = cols // 2

    qkv_half = lax.dynamic_slice_in_dim(w_qkv, core * half_depth, half_depth, 0).reshape(
        half_depth, 3 * cols
    )
    qkv_own = spread(qkv_half, "shard")
    qkv_other = swap(qkv_own, "ctx", 1)
    full_qkv = in_order(qkv_own, qkv_other, core, 1).reshape(width, 3 * cols)

    up_half = lax.dynamic_slice_in_dim(w_up, core * half_units, half_units, 1)
    down_half = lax.dynamic_slice_in_dim(w_down, core * half_units, half_units, 0).T
    out_half = lax.dynamic_slice_in_dim(w_out, core * half_cols, half_cols, 0).T
    batch = jnp.concatenate([up_half, down_half, out_half], 1)
    batch, _ = lax.optimization_barrier((batch, qkv_own))
    batch_all = spread(batch, "shard").reshape(width, 2 * half_units + half_cols)
    out_own = spread(batch_all[:, 2 * half_units :].T, "tp")
    out_other = swap(out_own, "ctx", 1)
    full_out = in_order(out_own, out_other, core, 1).reshape(parts * cols, width)
    ffn_near = batch_all[:, : 2 * half_units]
    ffn_far = swap(ffn_near, "tp", 2)
    near_other = swap(ffn_near, "ctx", 1)
    far_other = swap(ffn_far, "ctx", 1)
    ffn_parts = (ffn_near, near_other, ffn_far, far_other)
    full_up = jnp.concatenate([part[:, :half_units] for part in ffn_parts], 1)
    full_down = jnp.concatenate([part[:, half_units:] for part in ffn_parts], 1)
    bias_near = jnp.concatenate(
        [
            lax.dynamic_slice_in_dim(up_bias, core * half_units, half_units, 0),
            lax.dynamic_slice_in_dim(up_bias, (1 - core) * half_units, half_units, 0),
        ]
    )
    bias_pair = jnp.concatenate([bias_near, swap(bias_near, "tp", 2)])

    stream_in = tokens.astype(F32) + time_embed[:, None, :]
    stream_low = stream_in.astype(BF).reshape(rows, width)
    product = dot(stream_low, full_qkv, 1, 0).reshape(seqs, half_len, 3, cols)
    query_low = (product[:, :, 0] + qv_bias[0]).astype(BF)
    key_low = product[:, :, 1].astype(BF)
    value_low = (product[:, :, 2] + qv_bias[1]).astype(BF)
    pair_low = jnp.stack([key_low, value_low])
    pair_all = jnp.concatenate([pair_low, swap(pair_low, "ctx", 1)], 2)
    labels_own = lax.dynamic_slice_in_dim(segments, core * half_len, half_len, 1)
    labels_other = lax.dynamic_slice_in_dim(segments, (1 - core) * half_len, half_len, 1)
    labels_all = jnp.concatenate([labels_own, labels_other], 1)
    query_heads = query_low.reshape(seqs, half_len, heads, HD)
    key_heads = pair_all[0].reshape(seqs, 2 * half_len, heads, HD)
    value_heads = pair_all[1].reshape(seqs, 2 * half_len, heads, HD)
    heads_out, log_total = attend_forward(
        query_heads, key_heads, value_heads, labels_own, labels_all
    )
    heads_low = heads_out.astype(BF).reshape(seqs, parts, blk, cols)

    sent = jnp.stack(
        [jnp.stack([heads_low[:, i], heads_low[:, i ^ 1]]) for i in range(parts)]
    )
    heads_all = jnp.transpose(exchange(sent, "tp"), (1, 2, 3, 0, 4)).reshape(
        2 * own_rows, parts * cols
    )
    stream_blk = jnp.stack(
        [
            lax.dynamic_slice_in_dim(tokens, (place ^ i) * blk, blk, 1).astype(F32)
            + time_embed[:, None, :]
            for i in range(2)
        ]
    ).reshape(2 * own_rows, width)
    grad_blk = jnp.stack(
        [lax.dynamic_slice_in_dim(out_grad, (place ^ i) * blk, blk, 1) for i in range(2)]
    ).reshape(2 * own_rows, width)
    attn_out = dot(heads_all, full_out, 1, 0) + branch_bias[0]
    scaled_first, scale_first = norm_stats(stream_blk + attn_out)
    normed = scaled_first * norm_gains[0] + norm_shifts[0]
    normed_low = normed.astype(BF)
    pre_act = dot(normed_low, full_up, 1, 0) + bias_pair
    phi = 0.5 * (1.0 + lax.erf(pre_act * math.sqrt(0.5)))
    act_low = (pre_act * phi).astype(BF)
    slope = phi + pre_act * (jnp.exp(-0.5 * pre_act * pre_act) * (1.0 / math.sqrt(2.0 * math.pi)))
    down_part = dot(act_low, full_down, 1, 1)
    down_other = swap(down_part[own_rows:].astype(BF), "tp", 1)
    second_in = (
        normed[:own_rows] + down_part[:own_rows] + down_other.astype(F32) + branch_bias[1]
    ).astype(BF)
    second_all = jnp.concatenate([second_in, swap(second_in, "tp", 1)]).astype(F32)
    scaled_second, scale_second = norm_stats(second_all)
    layer_rows = (scaled_second * norm_gains[1] + norm_shifts[1]).astype(BF)
    layer_far = swap(layer_rows, "tp", 2)

    cotangent = grad_blk.astype(F32)
    grad_second = norm_grad(scaled_second, scale_second, cotangent, norm_gains[1])
    gain_second = jnp.sum((cotangent * scaled_second)[:own_rows], axis=0)
    shift_second = jnp.sum(cotangent[:own_rows], axis=0)
    bias_second = jnp.sum(grad_second[:own_rows], axis=0)
    grad_ffn_low = grad_second.astype(BF)
    grad_pre = dot(grad_ffn_low, full_down, 1, 0) * slope
    grad_pre_low = grad_pre.astype(BF)
    up_part = dot(grad_pre_low, full_up, 1, 1)
    up_other = swap(up_part[own_rows:].astype(BF), "tp", 1)
    grad_normed = up_part[:own_rows] + up_other.astype(F32) + grad_second[:own_rows]
    scaled_own = scaled_first[:own_rows]
    grad_first = norm_grad(scaled_own, scale_first[:own_rows], grad_normed, norm_gains[0])
    gain_first = jnp.sum(grad_normed * scaled_own, axis=0)
    shift_first = jnp.sum(grad_normed, axis=0)
    bias_first = jnp.sum(grad_first, axis=0)
    grad_attn_low = grad_first.astype(BF)
    grad_heads_own = dot(grad_attn_low, full_out, 1, 1).astype(BF)
    grad_heads = exchange(
        jnp.transpose(grad_heads_own.reshape(own_rows, parts, cols), (1, 0, 2)), "tp"
    )
    grad_heads = jnp.transpose(grad_heads.reshape(parts, seqs, blk, cols), (1, 0, 2, 3)).reshape(
        seqs, half_len, heads, HD
    )
    grad_query, grad_key_all, grad_value_all = attend_backward(
        query_heads, key_heads, value_heads, labels_own, labels_all, grad_heads, log_total
    )
    grad_pair = jnp.stack([grad_key_all, grad_value_all]).reshape(2, seqs, 2 * half_len, cols)
    grad_pair = grad_pair[:, :, :half_len] + swap(
        grad_pair[:, :, half_len:].astype(BF), "ctx", 1
    ).astype(F32)
    grad_query = grad_query.reshape(rows, cols)
    grad_key = grad_pair[0].reshape(rows, cols)
    grad_value = grad_pair[1].reshape(rows, cols)
    grad_prod_low = jnp.concatenate([grad_query, grad_key, grad_value], 1).astype(BF)
    qkv_part = dot(grad_prod_low, full_qkv, 1, 1).astype(BF)
    input_parts = exchange(
        jnp.transpose(qkv_part.reshape(seqs, parts, blk, width), (1, 0, 2, 3)), "tp"
    )
    input_own = jnp.sum(input_parts.astype(F32), axis=0) + grad_first.reshape(seqs, blk, width)
    input_all = spread(input_own.astype(BF), "tp")
    input_grad = jnp.transpose(input_all, (1, 0, 2, 3)).reshape(seqs, half_len, width).astype(F32)

    by_mask = jnp.concatenate(
        [layer_rows.reshape(2, seqs, blk, width), layer_far.reshape(2, seqs, blk, width)]
    )
    layer_out = jnp.stack(
        [lax.dynamic_index_in_dim(by_mask, place ^ i, 0, False) for i in range(parts)], 1
    )
    layer_out = layer_out.reshape(seqs, half_len, width).astype(F32)

    grad_up = dot(normed_low, grad_pre_low, 0, 0).astype(BF).reshape(width, 2, 2, half_units)
    grad_down = dot(grad_ffn_low, act_low, 0, 0).astype(BF).reshape(width, 2, 2, half_units)
    both = jnp.stack([grad_up, grad_down], 3)
    ffn_sum = both[:, :, 0].astype(F32) + swap(both[:, :, 1], "ctx", 1).astype(F32)
    ffn_sum = ffn_sum[:, 0] + swap(ffn_sum[:, 1].astype(BF), "tp", 2).astype(F32)
    ffn_sum = exchange(ffn_sum.astype(BF).reshape(deep, depth, 2 * half_units), "shard")
    ffn_sum = jnp.sum(ffn_sum.astype(F32), axis=0)
    ffn_both = in_order(
        ffn_sum.reshape(depth, 2, half_units),
        swap(ffn_sum, "ctx", 1).reshape(depth, 2, half_units),
        core,
        2,
    )
    up_share = ffn_both[:, 0]
    down_share = ffn_both[:, 1].T

    grad_out = dot(heads_all[:own_rows], grad_attn_low, 0, 0).astype(BF)
    grad_out = grad_out.reshape(parts, 2, half_cols, width)
    out_sum = lax.dynamic_index_in_dim(grad_out, core, 1, False).astype(F32) + swap(
        lax.dynamic_index_in_dim(grad_out, 1 - core, 1, False), "ctx", 1
    ).astype(F32)
    out_sum = jnp.sum(exchange(out_sum.astype(BF), "tp").astype(F32), axis=0)
    out_sum = jnp.transpose(out_sum.reshape(half_cols, deep, depth), (1, 2, 0))
    grad_qkv = dot(stream_low, grad_prod_low, 0, 0).astype(BF)
    grad_qkv = grad_qkv.reshape(deep, 2, half_depth, 3 * cols)
    qkv_sum = lax.dynamic_index_in_dim(grad_qkv, core, 1, False).astype(F32) + swap(
        lax.dynamic_index_in_dim(grad_qkv, 1 - core, 1, False), "ctx", 1
    ).astype(F32)
    qkv_sum = jnp.sum(exchange(qkv_sum.astype(BF), "shard").astype(F32), axis=0)
    qkv_share = in_order(qkv_sum, swap(qkv_sum, "ctx", 1), core, 0).reshape(depth, 3, cols)
    out_sum = jnp.sum(exchange(out_sum.astype(BF), "shard").astype(F32), axis=0)
    out_share = in_order(out_sum, swap(out_sum, "ctx", 1), core, 1).T

    norm_terms = jnp.concatenate(
        [gain_first, gain_second, shift_first, shift_second, bias_first, bias_second]
    )
    up_rel = jnp.sum(grad_pre, axis=0).reshape(2, 2, half_units)
    up_terms = in_order(up_rel[:, 0], up_rel[:, 1], core, 1)
    small = jnp.stack(
        [
            jnp.concatenate(
                [
                    norm_terms,
                    jnp.where(
                        place == i,
                        up_terms[0],
                        jnp.where(place == (i ^ 2), up_terms[1], 0.0),
                    ),
                ]
            )
            for i in range(parts)
        ]
    )
    small = jnp.sum(exchange(small, "tp"), axis=0)
    small = jnp.concatenate([small, jnp.sum(grad_query, axis=0), jnp.sum(grad_value, axis=0)])
    small = small + swap(small, "ctx", 1)
    small = jnp.sum(spread(small, "shard"), axis=0)
    norm_sum = small[: 6 * width].reshape(3, 2, width)
    up_sum = small[6 * width : 6 * width + units]
    qv_sum = small[6 * width + units :].reshape(2, cols)
    return (
        layer_out,
        input_grad,
        qkv_share,
        out_share,
        up_share,
        down_share,
        qv_sum,
        up_sum,
        norm_sum[0],
        norm_sum[1],
        norm_sum[2],
    )


def solution(mesh):
    placed = (
        P("shard", "ctx", None),
        P("shard", None),
        P("shard", None),
        P("shard", None, "tp"),
        P("tp", "shard"),
        P("shard", "tp"),
        P("tp", "shard"),
        P(None, "tp"),
        P("tp"),
        P(),
        P(),
        P(),
        P("shard", "ctx", None),
    )
    return jax.shard_map(
        shards,
        mesh=mesh,
        in_specs=placed,
        out_specs=(
            P("shard", "ctx", None),
            P("shard", "ctx", None),
            P("shard", None, "tp"),
            P("tp", "shard"),
            P("shard", "tp"),
            P("tp", "shard"),
            P(None, "tp"),
            P("tp"),
            P(),
            P(),
            P(),
        ),
        check_vma=False,
    )
```

```python
import math

import jax
import jax.numpy as jnp
from jax import lax
from jax.experimental import pallas as pl
from jax.experimental.pallas import tpu as pltpu
from jax.sharding import PartitionSpec as P

HD = 64
BF = jnp.bfloat16
F32 = jnp.float32
SCALE = HD**-0.5


def low(values):
    return lax.reduce_precision(values, 8, 7).astype(BF)


def dot(lhs, rhs, lhs_dim, rhs_dim):
    return lax.dot_general(
        lhs, rhs, (((lhs_dim,), (rhs_dim,)), ((), ())), preferred_element_type=F32
    )


def swap(values, axis, mask):
    size = lax.axis_size(axis)
    return lax.ppermute(values, axis, [(i, i ^ mask) for i in range(size)])


def gather_list(block, axis):
    return [block] + [swap(block, axis, m) for m in range(1, lax.axis_size(axis))]


def arrange(pieces, axis):
    index = lax.axis_index(axis)
    out = jnp.zeros((len(pieces), *pieces[0].shape), pieces[0].dtype)
    for m, piece in enumerate(pieces):
        out = lax.dynamic_update_index_in_dim(out, piece, index ^ m, 0)
    return out


def gather_ordered(block, axis):
    size = lax.axis_size(axis)
    if size <= 4:
        return arrange(gather_list(block, axis), axis)
    return lax.all_to_all(
        jnp.broadcast_to(block[None], (size, *block.shape)), axis, 0, 0, tiled=True
    )


def reduce_chunks(chunks, axis):
    size = lax.axis_size(axis)
    if size > 4:
        return jnp.sum(lax.all_to_all(chunks, axis, 0, 0, tiled=True).astype(F32), axis=0)
    index = lax.axis_index(axis)
    total = lax.dynamic_index_in_dim(chunks, index, 0, False).astype(F32)
    for m in range(1, size):
        sent = lax.dynamic_index_in_dim(chunks, index ^ m, 0, False)
        total = total + swap(sent, axis, m).astype(F32)
    return total


def in_order(own, other, index, dim):
    first = jnp.where(index == 0, own, other)
    second = jnp.where(index == 0, other, own)
    return jnp.concatenate([first, second], dim)


def norm_stats(residual):
    center = residual - jnp.mean(residual, axis=-1, keepdims=True)
    spread_of = jnp.mean(center * center, axis=-1, keepdims=True)
    scale = lax.rsqrt(spread_of + 1e-05)
    return center * scale, scale


def norm_grad(scaled, scale, grad, gain_vec):
    weighted = grad * gain_vec
    return scale * (
        weighted
        - jnp.mean(weighted, axis=-1, keepdims=True)
        - scaled * jnp.mean(weighted * scaled, axis=-1, keepdims=True)
    )


def _scores(query, key, same_doc):
    return jnp.where(same_doc, dot(key, query, 1, 1) * SCALE, -1e30)


def _forward_kernel(query_ref, own_ref, other_ref, lab_query_ref, lab_key_ref, heads_ref, log_ref):
    cols = query_ref.shape[2]
    same_doc = lab_key_ref[0] == lab_query_ref[0]
    pair = jnp.concatenate([own_ref[0], other_ref[0]], 0)
    outs = []
    logs = []
    for h in range(cols // HD):
        at = slice(h * HD, (h + 1) * HD)
        scores = _scores(query_ref[0][:, at], pair[:, at], same_doc)
        top = jnp.max(scores, axis=0, keepdims=True)
        exp_scores = jnp.exp(scores - top)
        total = jnp.sum(exp_scores, axis=0, keepdims=True)
        value = pair[:, cols + h * HD : cols + (h + 1) * HD]
        out = dot(value, exp_scores.astype(BF), 0, 0) / total
        outs.append(out)
        logs.append(top + jnp.log(total))
    heads_ref[0] = jnp.concatenate(outs, 0).T.astype(BF)
    log_ref[0] = jnp.concatenate(logs, 0)


def attend_forward(query, own, other, lab_query, lab_key):
    seqs, half_len, cols = query.shape
    blk = half_len // 2
    heads = cols // HD
    return pl.pallas_call(
        _forward_kernel,
        grid=(seqs, 2),
        in_specs=[
            pl.BlockSpec((1, blk, cols), lambda s, q: (s, q, 0)),
            pl.BlockSpec((1, half_len, 2 * cols), lambda s, q: (s, 0, 0)),
            pl.BlockSpec((1, half_len, 2 * cols), lambda s, q: (s, 0, 0)),
            pl.BlockSpec((1, 1, blk), lambda s, q: (s, 0, q)),
            pl.BlockSpec((1, 2 * half_len, 1), lambda s, q: (s, 0, 0)),
        ],
        out_specs=[
            pl.BlockSpec((1, blk, cols), lambda s, q: (s, q, 0)),
            pl.BlockSpec((1, heads, blk), lambda s, q: (s, 0, q)),
        ],
        out_shape=[
            jax.ShapeDtypeStruct((seqs, half_len, cols), BF),
            jax.ShapeDtypeStruct((seqs, heads, half_len), F32),
        ],
        name="attend_forward",
    )(query, own, other, lab_query, lab_key)


def _backward_kernel(
    query_ref, own_ref, other_ref, lab_query_ref, lab_key_ref, grad_ref, log_ref,
    grad_query_ref, grad_own_ref, grad_other_ref, sums_ref, key_acc, value_acc,
):
    cols = query_ref.shape[2]
    half_len = own_ref.shape[1]
    heads = cols // HD
    first = pl.program_id(1) == 0
    same_doc = lab_key_ref[0] == lab_query_ref[0]
    pair = jnp.concatenate([own_ref[0], other_ref[0]], 0)
    grads = []
    key_parts = []
    value_parts = []
    for h in range(heads):
        at = slice(h * HD, (h + 1) * HD)
        query = query_ref[0][:, at]
        key = pair[:, at]
        value = pair[:, cols + h * HD : cols + (h + 1) * HD]
        grad_out = grad_ref[0][:, at]
        probs = jnp.exp(_scores(query, key, same_doc) - log_ref[0, h : h + 1, :])
        grad_probs = dot(value, grad_out, 1, 1)
        inner = jnp.sum(probs * grad_probs, axis=0, keepdims=True)
        grad_scores = (probs * (grad_probs - inner)).astype(BF)
        value_parts.append(dot(probs.astype(BF), grad_out, 1, 0))
        key_parts.append(dot(grad_scores, query, 1, 0) * SCALE)
        grads.append(dot(key, grad_scores, 0, 0) * SCALE)
    grad_query = jnp.concatenate(grads, 0).T
    grad_query_ref[0] = grad_query.astype(BF)
    key_part = jnp.concatenate(key_parts, 1)
    value_part = jnp.concatenate(value_parts, 1)
    sums = jnp.concatenate(
        [
            jnp.sum(grad_query, axis=0, keepdims=True),
            jnp.sum(value_part, axis=0, keepdims=True),
        ],
        0,
    )

    @pl.when(first)
    def _():
        key_acc[...] = key_part
        value_acc[...] = value_part
        sums_ref[0] = sums

    @pl.when(jnp.logical_not(first))
    def _():
        key_all = key_acc[...] + key_part
        value_all = value_acc[...] + value_part
        both = jnp.concatenate([key_all, value_all], 1).astype(BF)
        grad_own_ref[0] = both[:half_len]
        grad_other_ref[0] = both[half_len:]
        sums_ref[0] = sums_ref[0] + sums


def attend_backward(query, own, other, lab_query, lab_key, grad_heads, logs):
    seqs, half_len, cols = query.shape
    blk = half_len // 2
    heads = cols // HD
    return pl.pallas_call(
        _backward_kernel,
        grid=(seqs, 2),
        in_specs=[
            pl.BlockSpec((1, blk, cols), lambda s, q: (s, q, 0)),
            pl.BlockSpec((1, half_len, 2 * cols), lambda s, q: (s, 0, 0)),
            pl.BlockSpec((1, half_len, 2 * cols), lambda s, q: (s, 0, 0)),
            pl.BlockSpec((1, 1, blk), lambda s, q: (s, 0, q)),
            pl.BlockSpec((1, 2 * half_len, 1), lambda s, q: (s, 0, 0)),
            pl.BlockSpec((1, blk, cols), lambda s, q: (s, q, 0)),
            pl.BlockSpec((1, heads, blk), lambda s, q: (s, 0, q)),
        ],
        out_specs=[
            pl.BlockSpec((1, blk, cols), lambda s, q: (s, q, 0)),
            pl.BlockSpec((1, half_len, 2 * cols), lambda s, q: (s, 0, 0)),
            pl.BlockSpec((1, half_len, 2 * cols), lambda s, q: (s, 0, 0)),
            pl.BlockSpec((1, 2, cols), lambda s, q: (s, 0, 0)),
        ],
        out_shape=[
            jax.ShapeDtypeStruct((seqs, half_len, cols), BF),
            jax.ShapeDtypeStruct((seqs, half_len, 2 * cols), BF),
            jax.ShapeDtypeStruct((seqs, half_len, 2 * cols), BF),
            jax.ShapeDtypeStruct((seqs, 2, cols), F32),
        ],
        scratch_shapes=[
            pltpu.VMEM((2 * half_len, cols), F32),
            pltpu.VMEM((2 * half_len, cols), F32),
        ],
        name="attend_backward",
    )(query, own, other, lab_query, lab_key, grad_heads, logs)


def shards(
    tokens,
    time_embed,
    segments,
    w_qkv,
    w_out,
    w_up,
    w_down,
    qv_bias,
    up_bias,
    norm_gains,
    norm_shifts,
    branch_bias,
    out_grad,
):
    seqs, half_len, width = tokens.shape
    parts = lax.axis_size("tp")
    deep = lax.axis_size("shard")
    core = lax.axis_index("ctx")
    place = lax.axis_index("tp")
    rows = seqs * half_len
    blk = half_len // parts
    own_rows = seqs * blk
    cols = w_qkv.shape[2]
    units = w_up.shape[1]
    half_units = units // 2
    depth = w_qkv.shape[0]
    half_depth = depth // 2
    half_cols = cols // 2

    w_kvq = jnp.concatenate([w_qkv[:, 1], w_qkv[:, 2], w_qkv[:, 0]], 1)
    kvq_half = lax.dynamic_slice_in_dim(w_kvq, core * half_depth, half_depth, 0)
    out_half = lax.dynamic_slice_in_dim(w_out, core * half_cols, half_cols, 0)
    if half_cols == half_depth:
        front_own = gather_ordered(jnp.concatenate([kvq_half, out_half], 1), "shard")
        kvq_own, out_gathered = front_own[:, :, : 3 * cols], front_own[:, :, 3 * cols :]
    else:
        front_own = kvq_own = gather_ordered(kvq_half, "shard")
        out_gathered = gather_ordered(out_half, "shard")
    kvq_other = swap(kvq_own, "ctx", 1)
    full_kvq = in_order(kvq_own, kvq_other, core, 1).reshape(width, 3 * cols)

    up_half = lax.dynamic_slice_in_dim(w_up, core * half_units, half_units, 1)
    down_half = lax.dynamic_slice_in_dim(w_down, core * half_units, half_units, 0).T
    batch = jnp.concatenate([up_half, down_half], 1)
    batch, _ = lax.optimization_barrier((batch, front_own))
    if deep <= 4:
        near_list = gather_list(batch, "shard")
        far_list = [swap(piece, "tp", 2) for piece in near_list]
        ffn_near = arrange(near_list, "shard").reshape(width, 2 * half_units)
        ffn_far = arrange(far_list, "shard").reshape(width, 2 * half_units)
    else:
        ffn_near = gather_ordered(batch, "shard").reshape(width, 2 * half_units)
        ffn_far = swap(ffn_near, "tp", 2)
    near_other = swap(ffn_near, "ctx", 1)
    far_other = swap(ffn_far, "ctx", 1)
    ffn_parts = (ffn_near, ffn_far, near_other, far_other)
    full_up = jnp.concatenate([part[:, :half_units] for part in ffn_parts], 1)
    full_down = jnp.concatenate([part[:, half_units:] for part in ffn_parts], 1)
    bias_halves = up_bias.reshape(2, half_units)
    bias_near = jnp.where(core == 0, bias_halves, bias_halves[::-1])
    bias_far = swap(bias_near, "tp", 2)
    bias_pair = jnp.stack([bias_near, bias_far], 1).reshape(2 * units)

    stream_in = tokens.astype(F32) + time_embed[:, None, :]
    stream_low = stream_in.astype(BF).reshape(rows, width)
    kv_bias = jnp.concatenate([jnp.zeros_like(qv_bias[1]), qv_bias[1]])
    pair_own = (dot(stream_low, full_kvq[:, : 2 * cols], 1, 0) + kv_bias).astype(BF)
    pair_own = pair_own.reshape(seqs, half_len, 2 * cols)
    pair_other = swap(pair_own, "ctx", 1)
    query = (dot(stream_low, full_kvq[:, 2 * cols :], 1, 0) + qv_bias[0]).astype(BF)
    query = query.reshape(seqs, half_len, cols)
    labels_own = lax.dynamic_slice_in_dim(segments, core * half_len, half_len, 1)
    labels_other = lax.dynamic_slice_in_dim(segments, (1 - core) * half_len, half_len, 1)
    lab_query = labels_own[:, None, :]
    lab_key = jnp.concatenate([labels_own, labels_other], 1)[:, :, None]
    with jax.named_scope("attn_fwd"):
        heads_low, logs = attend_forward(query, pair_own, pair_other, lab_query, lab_key)

    out_rows = jnp.transpose(out_gathered, (1, 0, 2)).reshape(half_cols, width)
    out_own = jnp.stack(gather_list(out_rows, "tp"))
    out_other = swap(out_own, "ctx", 1)
    full_out = in_order(out_own, out_other, core, 1).reshape(parts * cols, width)

    def block_of(values, m):
        return lax.dynamic_slice_in_dim(values, (place ^ m) * blk, blk, 1)

    heads_sent = [
        jnp.stack([block_of(heads_low, m), block_of(heads_low, m ^ 1)]) for m in range(parts)
    ]
    heads_parts = [heads_sent[0]] + [swap(heads_sent[m], "tp", m) for m in range(1, parts)]
    heads_parts = [part.reshape(2, own_rows, cols) for part in heads_parts]

    def feed_forward(side):
        stream = (block_of(tokens, side).astype(F32) + time_embed[:, None, :]).reshape(
            own_rows, width
        )
        heads_all = jnp.concatenate([part[side] for part in heads_parts], 1)
        attn_out = dot(heads_all, full_out, 1, 0) + branch_bias[0]
        scaled, scale = norm_stats(stream + attn_out)
        normed = scaled * norm_gains[0] + norm_shifts[0]
        normed_low = normed.astype(BF)
        pre_act = dot(normed_low, full_up, 1, 0) + bias_pair
        phi = 0.5 * (1.0 + lax.erf(pre_act * math.sqrt(0.5)))
        act_low = (pre_act * phi).astype(BF)
        slope = phi + pre_act * (
            jnp.exp(-0.5 * pre_act * pre_act) * (1.0 / math.sqrt(2.0 * math.pi))
        )
        return heads_all, scaled, scale, normed, normed_low, act_low, slope.astype(BF)

    def feed_backward(side, second_in, slope):
        cotangent = block_of(out_grad, side).astype(F32).reshape(own_rows, width)
        scaled, scale = norm_stats(second_in)
        grad_second = norm_grad(scaled, scale, cotangent, norm_gains[1])
        grad_ffn_low = grad_second.astype(BF)
        grad_pre = dot(grad_ffn_low, full_down, 1, 0) * slope.astype(F32)
        grad_pre_low = grad_pre.astype(BF)
        up_part = dot(grad_pre_low, full_up, 1, 1)
        return cotangent, scaled, grad_second, grad_ffn_low, grad_pre, grad_pre_low, up_part

    mate = feed_forward(1)
    down_mate = dot(mate[5], full_down, 1, 1).astype(BF)
    down_other = swap(down_mate, "tp", 1)
    own = feed_forward(0)
    heads_all, scaled_first, scale_first, normed, normed_low, act_low, slope = own
    down_part = dot(act_low, full_down, 1, 1)
    second_in = low(normed + down_part + down_other.astype(F32) + branch_bias[1])
    second_mate = swap(second_in, "tp", 1)
    (
        cotangent, scaled_second, grad_second, grad_ffn_low, grad_pre, grad_pre_low, up_part,
    ) = feed_backward(0, second_in.astype(F32), slope)
    (
        _, _, _, grad_ffn_mate, grad_pre_mate, grad_pre_low_mate, up_part_mate,
    ) = feed_backward(1, second_mate.astype(F32), mate[6])
    up_other = swap(up_part_mate.astype(BF), "tp", 1)
    scaled_both, _ = norm_stats(jnp.concatenate([second_in, second_mate]).astype(F32))
    layer_rows = low(scaled_both * norm_gains[1] + norm_shifts[1]).reshape(2, own_rows, width)
    layer_far = swap(layer_rows, "tp", 2)

    both_normed = jnp.concatenate([normed_low, mate[4]])
    both_pre = jnp.concatenate([grad_pre_low, grad_pre_low_mate])
    both_grad = jnp.concatenate([grad_ffn_low, grad_ffn_mate])
    both_act = jnp.concatenate([act_low, mate[5]])
    up_sent = dot(both_normed, both_pre[:, units:], 0, 0).astype(BF)
    down_sent = dot(both_grad, both_act[:, units:], 0, 0).astype(BF)
    up_got = swap(up_sent, "ctx", 1)
    down_got = swap(down_sent, "ctx", 1)
    up_sum = dot(both_normed, both_pre[:, :units], 0, 0) + up_got.astype(F32)
    down_sum = dot(both_grad, both_act[:, :units], 0, 0) + down_got.astype(F32)
    far_sum = jnp.concatenate([up_sum[:, half_units:], down_sum[:, half_units:]], 1).astype(BF)
    with jax.named_scope("far_grads"):
        far_got = swap(far_sum, "tp", 2)

    grad_normed = up_part + up_other.astype(F32) + grad_second
    grad_first = norm_grad(scaled_first, scale_first, grad_normed, norm_gains[0])
    grad_attn_low = grad_first.astype(BF)
    grad_heads_own = dot(grad_attn_low, full_out, 1, 1).astype(BF)
    grad_parts = [grad_heads_own[:, m * cols : (m + 1) * cols] for m in range(parts)]
    grad_parts = [grad_parts[0]] + [swap(grad_parts[m], "tp", m) for m in range(1, parts)]
    grad_heads = jnp.zeros((seqs, parts, blk, cols), BF)
    for m in range(parts):
        grad_heads = lax.dynamic_update_index_in_dim(
            grad_heads, grad_parts[m].reshape(seqs, blk, cols), place ^ m, 1
        )
    grad_heads = grad_heads.reshape(seqs, half_len, cols)
    with jax.named_scope("attn_bwd"):
        grad_query, grad_pair_own, grad_pair_other, sums = attend_backward(
            query, pair_own, pair_other, lab_query, lab_key, grad_heads, logs
        )
    grad_pair = (grad_pair_own.astype(F32) + swap(grad_pair_other, "ctx", 1).astype(F32)).astype(BF)
    grad_prod_low = jnp.concatenate([grad_pair, grad_query], 2).reshape(rows, 3 * cols)
    qkv_part = dot(grad_prod_low, full_kvq, 1, 1).astype(BF).reshape(seqs, parts, blk, width)
    input_own = grad_first.reshape(seqs, blk, width) + lax.dynamic_index_in_dim(
        qkv_part, place, 1, False
    ).astype(F32)
    for m in range(1, parts):
        sent = lax.dynamic_index_in_dim(qkv_part, place ^ m, 1, False)
        input_own = input_own + swap(sent, "tp", m).astype(F32)
    input_list = gather_list(low(input_own), "tp")

    def lay_out(blocks):
        out = jnp.zeros((seqs, parts, blk, width), F32)
        for m, block in enumerate(blocks):
            out = lax.dynamic_update_index_in_dim(
                out, block.astype(F32).reshape(seqs, blk, width), place ^ m, 1
            )
        return out.reshape(seqs, half_len, width)

    input_grad = lay_out(input_list)
    layer_out = lay_out([layer_rows[0], layer_rows[1], layer_far[0], layer_far[1]])

    near_sum = jnp.concatenate([up_sum[:, :half_units], down_sum[:, :half_units]], 1)
    ffn_sum = (near_sum + far_got.astype(F32)).astype(BF)
    ffn_sum = reduce_chunks(ffn_sum.reshape(deep, depth, 2 * half_units), "shard")
    ffn_sum = low(ffn_sum)
    ffn_both = in_order(
        ffn_sum.reshape(depth, 2, half_units),
        swap(ffn_sum, "ctx", 1).reshape(depth, 2, half_units),
        core,
        2,
    ).astype(F32)
    up_share = ffn_both[:, 0]
    down_share = ffn_both[:, 1].T

    grad_out = dot(heads_all, grad_attn_low, 0, 0).astype(BF).reshape(parts, 2, half_cols, width)
    out_sum = lax.dynamic_index_in_dim(grad_out, core, 1, False).astype(F32) + swap(
        lax.dynamic_index_in_dim(grad_out, 1 - core, 1, False), "ctx", 1
    ).astype(F32)
    out_low = out_sum.astype(BF)
    out_sum = out_sum[0]
    for m in range(1, parts):
        out_sum = out_sum + swap(out_low[m], "tp", m).astype(F32)
    out_chunks = jnp.transpose(out_sum.reshape(half_cols, deep, depth), (1, 0, 2)).astype(BF)
    grad_qkv = dot(stream_low, grad_prod_low, 0, 0).astype(BF)
    grad_qkv = grad_qkv.reshape(deep, 2, half_depth, 3 * cols)
    qkv_sum = lax.dynamic_index_in_dim(grad_qkv, core, 1, False).astype(F32) + swap(
        lax.dynamic_index_in_dim(grad_qkv, 1 - core, 1, False), "ctx", 1
    ).astype(F32)
    if half_cols == half_depth:
        front_sum = reduce_chunks(jnp.concatenate([qkv_sum.astype(BF), out_chunks], 2), "shard")
        front_sum = low(front_sum)
        front_both = in_order(front_sum, swap(front_sum, "ctx", 1), core, 0).astype(F32)
        kvq_share, out_share = front_both[:, : 3 * cols], front_both[:, 3 * cols :]
    else:
        qkv_sum = reduce_chunks(qkv_sum.astype(BF), "shard")
        out_sum = reduce_chunks(out_chunks, "shard")
        kvq_share = in_order(qkv_sum, swap(qkv_sum, "ctx", 1), core, 0)
        out_share = in_order(out_sum, swap(out_sum, "ctx", 1), core, 0)
    kvq_share = kvq_share.reshape(depth, 3, cols)
    qkv_share = jnp.stack([kvq_share[:, 2], kvq_share[:, 0], kvq_share[:, 1]], 1)

    norm_terms = jnp.concatenate(
        [
            jnp.sum(grad_normed * scaled_first, axis=0),
            jnp.sum(cotangent * scaled_second, axis=0),
            jnp.sum(grad_normed, axis=0),
            jnp.sum(cotangent, axis=0),
            jnp.sum(grad_first, axis=0),
            jnp.sum(grad_second, axis=0),
        ]
    )
    up_rel = (jnp.sum(grad_pre, axis=0) + jnp.sum(grad_pre_mate, axis=0)).reshape(
        2, 2, half_units
    )
    up_terms = in_order(up_rel[0], up_rel[1], core, 1)
    got = swap(jnp.concatenate([norm_terms, up_terms[1]]), "tp", 2)
    norm_terms = norm_terms + got[: 6 * width]
    norm_terms = norm_terms + swap(norm_terms, "tp", 1)
    small = jnp.concatenate(
        [norm_terms, up_terms[0] + got[6 * width :], jnp.sum(sums, axis=0).reshape(2 * cols)]
    )
    small = small + swap(small, "ctx", 1)
    step = 1
    while step < deep:
        small = small + swap(small, "shard", step)
        step *= 2
    norm_sum = small[: 6 * width].reshape(3, 2, width)
    up_total = small[6 * width : 6 * width + units]
    qv_sum = small[6 * width + units :].reshape(2, cols)
    return (
        layer_out,
        input_grad,
        qkv_share,
        out_share,
        up_share,
        down_share,
        qv_sum,
        up_total,
        norm_sum[0],
        norm_sum[1],
        norm_sum[2],
    )


def solution(mesh):
    placed = (
        P("shard", "ctx", None),
        P("shard", None),
        P("shard", None),
        P("shard", None, "tp"),
        P("tp", "shard"),
        P("shard", "tp"),
        P("tp", "shard"),
        P(None, "tp"),
        P("tp"),
        P(),
        P(),
        P(),
        P("shard", "ctx", None),
    )
    return jax.shard_map(
        shards,
        mesh=mesh,
        in_specs=placed,
        out_specs=(
            P("shard", "ctx", None),
            P("shard", "ctx", None),
            P("shard", None, "tp"),
            P("tp", "shard"),
            P("shard", "tp"),
            P("tp", "shard"),
            P(None, "tp"),
            P("tp"),
            P(),
            P(),
            P(),
        ),
        check_vma=False,
    )
```

```python
import math

import jax
import jax.numpy as jnp
from jax import lax
from jax.experimental import pallas as pl
from jax.experimental.pallas import tpu as pltpu
from jax.sharding import PartitionSpec as P


HD = 64
BF = jnp.bfloat16
F32 = jnp.float32
SCALE = HD**-0.5


def low(values):
    return lax.reduce_precision(values, 8, 7).astype(BF)


def dot(lhs, rhs, lhs_dim, rhs_dim):
    return lax.dot_general(
        lhs, rhs, (((lhs_dim,), (rhs_dim,)), ((), ())), preferred_element_type=F32
    )


def swap(values, axis, mask):
    size = lax.axis_size(axis)
    return lax.ppermute(values, axis, [(i, i ^ mask) for i in range(size)])


def gather_list(block, axis):
    return [block] + [swap(block, axis, m) for m in range(1, lax.axis_size(axis))]


def arrange(pieces, axis):
    index = lax.axis_index(axis)
    out = jnp.zeros((len(pieces), *pieces[0].shape), pieces[0].dtype)
    for m, piece in enumerate(pieces):
        out = lax.dynamic_update_index_in_dim(out, piece, index ^ m, 0)
    return out


def gather_ordered(block, axis):
    size = lax.axis_size(axis)
    if size <= 4:
        return arrange(gather_list(block, axis), axis)
    return lax.all_to_all(
        jnp.broadcast_to(block[None], (size, *block.shape)), axis, 0, 0, tiled=True
    )


def reduce_chunks(chunks, axis):
    size = lax.axis_size(axis)
    if size > 4:
        return jnp.sum(lax.all_to_all(chunks, axis, 0, 0, tiled=True).astype(F32), axis=0)
    index = lax.axis_index(axis)
    total = lax.dynamic_index_in_dim(chunks, index, 0, False).astype(F32)
    for m in range(1, size):
        sent = lax.dynamic_index_in_dim(chunks, index ^ m, 0, False)
        total = total + swap(sent, axis, m).astype(F32)
    return total


def in_order(own, other, index, dim):
    first = jnp.where(index == 0, own, other)
    second = jnp.where(index == 0, other, own)
    return jnp.concatenate([first, second], dim)


def norm_stats(residual):
    center = residual - jnp.mean(residual, axis=-1, keepdims=True)
    spread_of = jnp.mean(center * center, axis=-1, keepdims=True)
    scale = lax.rsqrt(spread_of + 1e-05)
    return center * scale, scale


def norm_grad(scaled, scale, grad, gain_vec):
    weighted = grad * gain_vec
    return scale * (
        weighted
        - jnp.mean(weighted, axis=-1, keepdims=True)
        - scaled * jnp.mean(weighted * scaled, axis=-1, keepdims=True)
    )


def _scores(query, key, same_doc):
    return jnp.where(same_doc, dot(key, query, 1, 1) * SCALE, -1e30)


def _forward_kernel(query_ref, own_ref, other_ref, lab_query_ref, lab_key_ref, heads_ref, log_ref):
    cols = query_ref.shape[2]
    same_doc = lab_key_ref[0] == lab_query_ref[0]
    pair = jnp.concatenate([own_ref[0], other_ref[0]], 0)
    outs = []
    logs = []
    for h in range(cols // HD):
        at = slice(h * HD, (h + 1) * HD)
        scores = _scores(query_ref[0][:, at], pair[:, at], same_doc)
        top = jnp.max(scores, axis=0, keepdims=True)
        exp_scores = jnp.exp(scores - top)
        total = jnp.sum(exp_scores, axis=0, keepdims=True)
        value = pair[:, cols + h * HD : cols + (h + 1) * HD]
        out = dot(value, exp_scores.astype(BF), 0, 0) / total
        outs.append(out)
        logs.append(top + jnp.log(total))
    heads_ref[0] = jnp.concatenate(outs, 0).T.astype(BF)
    log_ref[0] = jnp.concatenate(logs, 0)


def attend_forward(query, own, other, lab_query, lab_key):
    seqs, half_len, cols = query.shape
    blk = half_len // 2
    heads = cols // HD
    return pl.pallas_call(
        _forward_kernel,
        grid=(seqs, 2),
        in_specs=[
            pl.BlockSpec((1, blk, cols), lambda s, q: (s, q, 0)),
            pl.BlockSpec((1, half_len, 2 * cols), lambda s, q: (s, 0, 0)),
            pl.BlockSpec((1, half_len, 2 * cols), lambda s, q: (s, 0, 0)),
            pl.BlockSpec((1, 1, blk), lambda s, q: (s, 0, q)),
            pl.BlockSpec((1, 2 * half_len, 1), lambda s, q: (s, 0, 0)),
        ],
        out_specs=[
            pl.BlockSpec((1, blk, cols), lambda s, q: (s, q, 0)),
            pl.BlockSpec((1, heads, blk), lambda s, q: (s, 0, q)),
        ],
        out_shape=[
            jax.ShapeDtypeStruct((seqs, half_len, cols), BF),
            jax.ShapeDtypeStruct((seqs, heads, half_len), F32),
        ],
        name="attend_forward",
    )(query, own, other, lab_query, lab_key)


def _backward_kernel(
    query_ref, own_ref, other_ref, lab_query_ref, lab_key_ref, grad_ref, log_ref,
    grad_query_ref, grad_own_ref, grad_other_ref, sums_ref, key_acc, value_acc,
):
    cols = query_ref.shape[2]
    half_len = own_ref.shape[1]
    heads = cols // HD
    first = pl.program_id(1) == 0
    same_doc = lab_key_ref[0] == lab_query_ref[0]
    pair = jnp.concatenate([own_ref[0], other_ref[0]], 0)
    grads = []
    key_parts = []
    value_parts = []
    for h in range(heads):
        at = slice(h * HD, (h + 1) * HD)
        query = query_ref[0][:, at]
        key = pair[:, at]
        value = pair[:, cols + h * HD : cols + (h + 1) * HD]
        grad_out = grad_ref[0][:, at]
        probs = jnp.exp(_scores(query, key, same_doc) - log_ref[0, h : h + 1, :])
        grad_probs = dot(value, grad_out, 1, 1)
        inner = jnp.sum(probs * grad_probs, axis=0, keepdims=True)
        grad_scores = (probs * (grad_probs - inner)).astype(BF)
        value_parts.append(dot(probs.astype(BF), grad_out, 1, 0))
        key_parts.append(dot(grad_scores, query, 1, 0) * SCALE)
        grads.append(dot(key, grad_scores, 0, 0) * SCALE)
    grad_query = jnp.concatenate(grads, 0).T
    grad_query_ref[0] = grad_query.astype(BF)
    key_part = jnp.concatenate(key_parts, 1)
    value_part = jnp.concatenate(value_parts, 1)
    sums = jnp.concatenate(
        [
            jnp.sum(grad_query, axis=0, keepdims=True),
            jnp.sum(value_part, axis=0, keepdims=True),
        ],
        0,
    )

    @pl.when(first)
    def _():
        key_acc[...] = key_part
        value_acc[...] = value_part
        sums_ref[0] = sums

    @pl.when(jnp.logical_not(first))
    def _():
        key_all = key_acc[...] + key_part
        value_all = value_acc[...] + value_part
        both = jnp.concatenate([key_all, value_all], 1).astype(BF)
        grad_own_ref[0] = both[:half_len]
        grad_other_ref[0] = both[half_len:]
        sums_ref[0] = sums_ref[0] + sums


def attend_backward(query, own, other, lab_query, lab_key, grad_heads, logs):
    seqs, half_len, cols = query.shape
    blk = half_len // 2
    heads = cols // HD
    return pl.pallas_call(
        _backward_kernel,
        grid=(seqs, 2),
        in_specs=[
            pl.BlockSpec((1, blk, cols), lambda s, q: (s, q, 0)),
            pl.BlockSpec((1, half_len, 2 * cols), lambda s, q: (s, 0, 0)),
            pl.BlockSpec((1, half_len, 2 * cols), lambda s, q: (s, 0, 0)),
            pl.BlockSpec((1, 1, blk), lambda s, q: (s, 0, q)),
            pl.BlockSpec((1, 2 * half_len, 1), lambda s, q: (s, 0, 0)),
            pl.BlockSpec((1, blk, cols), lambda s, q: (s, q, 0)),
            pl.BlockSpec((1, heads, blk), lambda s, q: (s, 0, q)),
        ],
        out_specs=[
            pl.BlockSpec((1, blk, cols), lambda s, q: (s, q, 0)),
            pl.BlockSpec((1, half_len, 2 * cols), lambda s, q: (s, 0, 0)),
            pl.BlockSpec((1, half_len, 2 * cols), lambda s, q: (s, 0, 0)),
            pl.BlockSpec((1, 2, cols), lambda s, q: (s, 0, 0)),
        ],
        out_shape=[
            jax.ShapeDtypeStruct((seqs, half_len, cols), BF),
            jax.ShapeDtypeStruct((seqs, half_len, 2 * cols), BF),
            jax.ShapeDtypeStruct((seqs, half_len, 2 * cols), BF),
            jax.ShapeDtypeStruct((seqs, 2, cols), F32),
        ],
        scratch_shapes=[
            pltpu.VMEM((2 * half_len, cols), F32),
            pltpu.VMEM((2 * half_len, cols), F32),
        ],
        name="attend_backward",
    )(query, own, other, lab_query, lab_key, grad_heads, logs)


def shards(
    tokens,
    time_embed,
    segments,
    w_qkv,
    w_out,
    w_up,
    w_down,
    qv_bias,
    up_bias,
    norm_gains,
    norm_shifts,
    branch_bias,
    out_grad,
):
    seqs, half_len, width = tokens.shape
    parts = lax.axis_size("tp")
    deep = lax.axis_size("shard")
    core = lax.axis_index("ctx")
    place = lax.axis_index("tp")
    rows = seqs * half_len
    blk = half_len // parts
    own_rows = seqs * blk
    cols = w_qkv.shape[2]
    units = w_up.shape[1]
    half_units = units // 2
    depth = w_qkv.shape[0]
    half_depth = depth // 2
    half_cols = cols // 2

    w_kvq = jnp.concatenate([w_qkv[:, 1], w_qkv[:, 2], w_qkv[:, 0]], 1)
    kvq_half = lax.dynamic_slice_in_dim(w_kvq, core * half_depth, half_depth, 0)
    out_half = lax.dynamic_slice_in_dim(w_out, core * half_cols, half_cols, 0)
    if half_cols == half_depth:
        front_own = gather_ordered(jnp.concatenate([kvq_half, out_half], 1), "shard")
        kvq_own, out_gathered = front_own[:, :, : 3 * cols], front_own[:, :, 3 * cols :]
    else:
        front_own = kvq_own = gather_ordered(kvq_half, "shard")
        out_gathered = gather_ordered(out_half, "shard")
    kvq_other = swap(kvq_own, "ctx", 1)
    full_kvq = in_order(kvq_own, kvq_other, core, 1).reshape(width, 3 * cols)

    up_half = lax.dynamic_slice_in_dim(w_up, core * half_units, half_units, 1)
    down_half = lax.dynamic_slice_in_dim(w_down, core * half_units, half_units, 0).T
    batch = jnp.concatenate([up_half, down_half], 1)
    batch, _ = lax.optimization_barrier((batch, front_own))
    if deep <= 4:
        near_list = gather_list(batch, "shard")
        far_list = [swap(piece, "tp", 2) for piece in near_list[:2]]
    bias_halves = up_bias.reshape(2, half_units)
    bias_near = jnp.where(core == 0, bias_halves, bias_halves[::-1])
    bias_far = swap(bias_near, "tp", 2)
    bias_pair = jnp.stack([bias_near, bias_far], 1).reshape(2 * units)

    stream_in = tokens.astype(F32) + time_embed[:, None, :]
    stream_low = stream_in.astype(BF).reshape(rows, width)
    kv_bias = jnp.concatenate([jnp.zeros_like(qv_bias[1]), qv_bias[1]])
    pair_own = (dot(stream_low, full_kvq[:, : 2 * cols], 1, 0) + kv_bias).astype(BF)
    pair_own = pair_own.reshape(seqs, half_len, 2 * cols)
    pair_other = swap(pair_own, "ctx", 1)
    query = (dot(stream_low, full_kvq[:, 2 * cols :], 1, 0) + qv_bias[0]).astype(BF)
    query = query.reshape(seqs, half_len, cols)
    labels_own = lax.dynamic_slice_in_dim(segments, core * half_len, half_len, 1)
    labels_other = lax.dynamic_slice_in_dim(segments, (1 - core) * half_len, half_len, 1)
    lab_query = labels_own[:, None, :]
    lab_key = jnp.concatenate([labels_own, labels_other], 1)[:, :, None]
    heads_low, logs = attend_forward(query, pair_own, pair_other, lab_query, lab_key)

    if deep <= 4:
        *held, _ = lax.optimization_barrier((*near_list, *far_list, heads_low))
        near_list, far_list = held[:deep], held[deep:]
        far_list = far_list + [swap(piece, "tp", 2) for piece in near_list[2:]]
        ffn_near = arrange(near_list, "shard").reshape(width, 2 * half_units)
        ffn_far = arrange(far_list, "shard").reshape(width, 2 * half_units)
    else:
        ffn_near = gather_ordered(batch, "shard").reshape(width, 2 * half_units)
        ffn_far = swap(ffn_near, "tp", 2)
    near_other = swap(ffn_near, "ctx", 1)
    far_other = swap(ffn_far, "ctx", 1)
    ffn_parts = (ffn_near, ffn_far, near_other, far_other)
    full_up = jnp.concatenate([part[:, :half_units] for part in ffn_parts], 1)
    full_down = jnp.concatenate([part[:, half_units:] for part in ffn_parts], 1)

    out_rows = jnp.transpose(out_gathered, (1, 0, 2)).reshape(half_cols, width)
    out_own = jnp.stack(gather_list(out_rows, "tp"))
    out_other = swap(out_own, "ctx", 1)
    full_out = in_order(out_own, out_other, core, 1).reshape(parts * cols, width)

    def block_of(values, m):
        return lax.dynamic_slice_in_dim(values, (place ^ m) * blk, blk, 1)

    heads_sent = [
        jnp.stack([block_of(heads_low, m), block_of(heads_low, m ^ 1)]) for m in range(parts)
    ]
    heads_parts = [heads_sent[0]] + [swap(heads_sent[m], "tp", m) for m in range(1, parts)]
    heads_parts = [part.reshape(2, own_rows, cols) for part in heads_parts]

    def feed_forward(side):
        stream = (block_of(tokens, side).astype(F32) + time_embed[:, None, :]).reshape(
            own_rows, width
        )
        heads_all = jnp.concatenate([part[side] for part in heads_parts], 1)
        attn_out = dot(heads_all, full_out, 1, 0) + branch_bias[0]
        scaled, scale = norm_stats(stream + attn_out)
        normed = scaled * norm_gains[0] + norm_shifts[0]
        normed_low = normed.astype(BF)
        pre_act = dot(normed_low, full_up, 1, 0) + bias_pair
        phi = 0.5 * (1.0 + lax.erf(pre_act * math.sqrt(0.5)))
        act_low = (pre_act * phi).astype(BF)
        slope = phi + pre_act * (
            jnp.exp(-0.5 * pre_act * pre_act) * (1.0 / math.sqrt(2.0 * math.pi))
        )
        return heads_all, scaled, scale, normed, normed_low, act_low, slope.astype(BF)

    def feed_backward(side, second_in, slope):
        cotangent = block_of(out_grad, side).astype(F32).reshape(own_rows, width)
        scaled, scale = norm_stats(second_in)
        grad_second = norm_grad(scaled, scale, cotangent, norm_gains[1])
        grad_ffn_low = grad_second.astype(BF)
        grad_pre = dot(grad_ffn_low, full_down, 1, 0) * slope.astype(F32)
        grad_pre_low = grad_pre.astype(BF)
        up_part = dot(grad_pre_low, full_up, 1, 1)
        return cotangent, scaled, grad_second, grad_ffn_low, grad_pre, grad_pre_low, up_part

    mate = feed_forward(1)
    down_mate = dot(mate[5], full_down, 1, 1).astype(BF)
    down_other = swap(down_mate, "tp", 1)
    own = feed_forward(0)
    heads_all, scaled_first, scale_first, normed, normed_low, act_low, slope = own
    down_part = dot(act_low, full_down, 1, 1)
    second_in = low(normed + down_part + down_other.astype(F32) + branch_bias[1])
    second_mate = swap(second_in, "tp", 1)
    (
        cotangent, scaled_second, grad_second, grad_ffn_low, grad_pre, grad_pre_low, up_part,
    ) = feed_backward(0, second_in.astype(F32), slope)
    (
        _, _, _, grad_ffn_mate, grad_pre_mate, grad_pre_low_mate, up_part_mate,
    ) = feed_backward(1, second_mate.astype(F32), mate[6])
    up_other = swap(up_part_mate.astype(BF), "tp", 1)
    scaled_both, _ = norm_stats(jnp.concatenate([second_in, second_mate]).astype(F32))
    layer_rows = low(scaled_both * norm_gains[1] + norm_shifts[1]).reshape(2, own_rows, width)
    layer_far = swap(layer_rows, "tp", 2)

    both_normed = jnp.concatenate([normed_low, mate[4]])
    both_pre = jnp.concatenate([grad_pre_low, grad_pre_low_mate])
    both_grad = jnp.concatenate([grad_ffn_low, grad_ffn_mate])
    both_act = jnp.concatenate([act_low, mate[5]])
    up_sent = dot(both_normed, both_pre[:, units:], 0, 0).astype(BF)
    down_sent = dot(both_grad, both_act[:, units:], 0, 0).astype(BF)
    up_got = swap(up_sent, "ctx", 1)
    down_got = swap(down_sent, "ctx", 1)
    up_sum = dot(both_normed, both_pre[:, :units], 0, 0) + up_got.astype(F32)
    down_sum = dot(both_grad, both_act[:, :units], 0, 0) + down_got.astype(F32)
    far_sum = jnp.concatenate([up_sum[:, half_units:], down_sum[:, half_units:]], 1).astype(BF)
    far_got = swap(far_sum, "tp", 2)

    grad_normed = up_part + up_other.astype(F32) + grad_second
    grad_first = norm_grad(scaled_first, scale_first, grad_normed, norm_gains[0])
    grad_attn_low = grad_first.astype(BF)
    grad_heads_own = dot(grad_attn_low, full_out, 1, 1).astype(BF)
    grad_parts = [grad_heads_own[:, m * cols : (m + 1) * cols] for m in range(parts)]
    grad_parts = [grad_parts[0]] + [swap(grad_parts[m], "tp", m) for m in range(1, parts)]
    grad_heads = jnp.zeros((seqs, parts, blk, cols), BF)
    for m in range(parts):
        grad_heads = lax.dynamic_update_index_in_dim(
            grad_heads, grad_parts[m].reshape(seqs, blk, cols), place ^ m, 1
        )
    grad_heads = grad_heads.reshape(seqs, half_len, cols)
    grad_heads, _ = lax.optimization_barrier((grad_heads, far_sum))
    grad_query, grad_pair_own, grad_pair_other, sums = attend_backward(
        query, pair_own, pair_other, lab_query, lab_key, grad_heads, logs
    )
    grad_pair = (grad_pair_own.astype(F32) + swap(grad_pair_other, "ctx", 1).astype(F32)).astype(BF)
    grad_prod_low = jnp.concatenate([grad_pair, grad_query], 2).reshape(rows, 3 * cols)
    qkv_part = dot(grad_prod_low, full_kvq, 1, 1).astype(BF).reshape(seqs, parts, blk, width)
    input_own = grad_first.reshape(seqs, blk, width) + lax.dynamic_index_in_dim(
        qkv_part, place, 1, False
    ).astype(F32)
    for m in range(1, parts):
        sent = lax.dynamic_index_in_dim(qkv_part, place ^ m, 1, False)
        input_own = input_own + swap(sent, "tp", m).astype(F32)
    near_sum = jnp.concatenate([up_sum[:, :half_units], down_sum[:, :half_units]], 1)
    ffn_sum = (near_sum + far_got.astype(F32)).astype(BF)
    input_low, _ = lax.optimization_barrier((low(input_own), ffn_sum))
    input_list = gather_list(input_low, "tp")

    def lay_out(blocks):
        out = jnp.zeros((seqs, parts, blk, width), F32)
        for m, block in enumerate(blocks):
            out = lax.dynamic_update_index_in_dim(
                out, block.astype(F32).reshape(seqs, blk, width), place ^ m, 1
            )
        return out.reshape(seqs, half_len, width)

    input_grad = lay_out(input_list)
    layer_out = lay_out([layer_rows[0], layer_rows[1], layer_far[0], layer_far[1]])

    ffn_sum = reduce_chunks(ffn_sum.reshape(deep, depth, 2 * half_units), "shard")
    ffn_sum = low(ffn_sum)
    ffn_both = in_order(
        ffn_sum.reshape(depth, 2, half_units),
        swap(ffn_sum, "ctx", 1).reshape(depth, 2, half_units),
        core,
        2,
    ).astype(F32)
    up_share = ffn_both[:, 0]
    down_share = ffn_both[:, 1].T

    grad_out = dot(heads_all, grad_attn_low, 0, 0).astype(BF).reshape(parts, 2, half_cols, width)
    out_sum = lax.dynamic_index_in_dim(grad_out, core, 1, False).astype(F32) + swap(
        lax.dynamic_index_in_dim(grad_out, 1 - core, 1, False), "ctx", 1
    ).astype(F32)
    out_low = out_sum.astype(BF)
    out_sum = out_sum[0]
    for m in range(1, parts):
        out_sum = out_sum + swap(out_low[m], "tp", m).astype(F32)
    out_chunks = jnp.transpose(out_sum.reshape(half_cols, deep, depth), (1, 0, 2)).astype(BF)
    grad_qkv = dot(stream_low, grad_prod_low, 0, 0).astype(BF)
    grad_qkv = grad_qkv.reshape(deep, 2, half_depth, 3 * cols)
    qkv_sum = lax.dynamic_index_in_dim(grad_qkv, core, 1, False).astype(F32) + swap(
        lax.dynamic_index_in_dim(grad_qkv, 1 - core, 1, False), "ctx", 1
    ).astype(F32)
    if half_cols == half_depth:
        front_sum = reduce_chunks(jnp.concatenate([qkv_sum.astype(BF), out_chunks], 2), "shard")
        front_sum = low(front_sum)
        front_both = in_order(front_sum, swap(front_sum, "ctx", 1), core, 0).astype(F32)
        kvq_share, out_share = front_both[:, : 3 * cols], front_both[:, 3 * cols :]
    else:
        qkv_sum = reduce_chunks(qkv_sum.astype(BF), "shard")
        out_sum = reduce_chunks(out_chunks, "shard")
        kvq_share = in_order(qkv_sum, swap(qkv_sum, "ctx", 1), core, 0)
        out_share = in_order(out_sum, swap(out_sum, "ctx", 1), core, 0)
    kvq_share = kvq_share.reshape(depth, 3, cols)
    qkv_share = jnp.stack([kvq_share[:, 2], kvq_share[:, 0], kvq_share[:, 1]], 1)

    norm_terms = jnp.concatenate(
        [
            jnp.sum(grad_normed * scaled_first, axis=0),
            jnp.sum(cotangent * scaled_second, axis=0),
            jnp.sum(grad_normed, axis=0),
            jnp.sum(cotangent, axis=0),
            jnp.sum(grad_first, axis=0),
            jnp.sum(grad_second, axis=0),
        ]
    )
    up_rel = (jnp.sum(grad_pre, axis=0) + jnp.sum(grad_pre_mate, axis=0)).reshape(
        2, 2, half_units
    )
    up_terms = in_order(up_rel[0], up_rel[1], core, 1)
    norm_terms, up_own, up_far, _ = lax.optimization_barrier(
        (norm_terms, up_terms[0], up_terms[1], qkv_part)
    )
    got = swap(jnp.concatenate([norm_terms, up_far]), "tp", 2)
    norm_terms = norm_terms + got[: 6 * width]
    norm_terms = norm_terms + swap(norm_terms, "tp", 1)
    small = jnp.concatenate(
        [norm_terms, up_own + got[6 * width :], jnp.sum(sums, axis=0).reshape(2 * cols)]
    )
    small = small + swap(small, "ctx", 1)
    step = 1
    while step < deep:
        small = small + swap(small, "shard", step)
        step *= 2
    norm_sum = small[: 6 * width].reshape(3, 2, width)
    up_total = small[6 * width : 6 * width + units]
    qv_sum = small[6 * width + units :].reshape(2, cols)
    return (
        layer_out,
        input_grad,
        qkv_share,
        out_share,
        up_share,
        down_share,
        qv_sum,
        up_total,
        norm_sum[0],
        norm_sum[1],
        norm_sum[2],
    )


def solution(mesh):
    placed = (
        P("shard", "ctx", None),
        P("shard", None),
        P("shard", None),
        P("shard", None, "tp"),
        P("tp", "shard"),
        P("shard", "tp"),
        P("tp", "shard"),
        P(None, "tp"),
        P("tp"),
        P(),
        P(),
        P(),
        P("shard", "ctx", None),
    )

    return jax.shard_map(
        shards,
        mesh=mesh,
        in_specs=placed,
        out_specs=(
            P("shard", "ctx", None),
            P("shard", "ctx", None),
            P("shard", None, "tp"),
            P("tp", "shard"),
            P("shard", "tp"),
            P("tp", "shard"),
            P(None, "tp"),
            P("tp"),
            P(),
            P(),
            P(),
        ),
        check_vma=False,
    )
```

```python
import math

import jax
import jax.numpy as jnp
from jax import lax
from jax.experimental import pallas as pl
from jax.experimental.pallas import tpu as pltpu
from jax.sharding import PartitionSpec as P


HD = 64
BF = jnp.bfloat16
F32 = jnp.float32
SCALE = HD**-0.5


def low(values):
    return lax.reduce_precision(values, 8, 7).astype(BF)


def dot(lhs, rhs, lhs_dim, rhs_dim):
    return lax.dot_general(
        lhs, rhs, (((lhs_dim,), (rhs_dim,)), ((), ())), preferred_element_type=F32
    )


def swap(values, axis, mask):
    size = lax.axis_size(axis)
    return lax.ppermute(values, axis, [(i, i ^ mask) for i in range(size)])


def gather_list(block, axis):
    return [block] + [swap(block, axis, m) for m in range(1, lax.axis_size(axis))]


def arrange(pieces, axis):
    index = lax.axis_index(axis)
    rows, cols = pieces[0].shape
    out = jnp.zeros((len(pieces) * rows, cols), pieces[0].dtype)
    for m, piece in enumerate(pieces):
        out = lax.dynamic_update_slice_in_dim(out, piece, (index ^ m) * rows, 0)
    return lax.optimization_barrier(out).reshape(len(pieces), rows, cols)


def gather_ordered(block, axis):
    size = lax.axis_size(axis)
    if size <= 4:
        return arrange(gather_list(block, axis), axis)
    return lax.all_to_all(
        jnp.broadcast_to(block[None], (size, *block.shape)), axis, 0, 0, tiled=True
    )


def reduce_chunks(chunks, axis):
    size = lax.axis_size(axis)
    if size > 4:
        return jnp.sum(lax.all_to_all(chunks, axis, 0, 0, tiled=True).astype(F32), axis=0)
    index = lax.axis_index(axis)
    total = lax.dynamic_index_in_dim(chunks, index, 0, False).astype(F32)
    for m in range(1, size):
        sent = lax.dynamic_index_in_dim(chunks, index ^ m, 0, False)
        total = total + swap(sent, axis, m).astype(F32)
    return total


def in_order(own, other, index, dim):
    first = jnp.where(index == 0, own, other)
    second = jnp.where(index == 0, other, own)
    return jnp.concatenate([first, second], dim)


def norm_stats(residual):
    center = residual - jnp.mean(residual, axis=-1, keepdims=True)
    spread_of = jnp.mean(center * center, axis=-1, keepdims=True)
    scale = lax.rsqrt(spread_of + 1e-05)
    return center * scale, scale


def norm_grad(scaled, scale, grad, gain_vec):
    weighted = grad * gain_vec
    return scale * (
        weighted
        - jnp.mean(weighted, axis=-1, keepdims=True)
        - scaled * jnp.mean(weighted * scaled, axis=-1, keepdims=True)
    )


def _scores(query, key, same_doc):
    return jnp.where(same_doc, dot(key, query, 1, 1) * SCALE, -1e30)


def _forward_kernel(query_ref, own_ref, other_ref, lab_query_ref, lab_key_ref, heads_ref, log_ref):
    cols = query_ref.shape[2]
    same_doc = lab_key_ref[0] == lab_query_ref[0]
    pair = jnp.concatenate([own_ref[0], other_ref[0]], 0)
    outs = []
    logs = []
    for h in range(cols // HD):
        at = slice(h * HD, (h + 1) * HD)
        scores = _scores(query_ref[0][:, at], pair[:, at], same_doc)
        top = jnp.max(scores, axis=0, keepdims=True)
        exp_scores = jnp.exp(scores - top)
        total = jnp.sum(exp_scores, axis=0, keepdims=True)
        value = pair[:, cols + h * HD : cols + (h + 1) * HD]
        out = dot(value, exp_scores.astype(BF), 0, 0) / total
        outs.append(out)
        logs.append(top + jnp.log(total))
    heads_ref[0] = jnp.concatenate(outs, 0).T.astype(BF)
    log_ref[0] = jnp.concatenate(logs, 0)


def attend_forward(query, own, other, lab_query, lab_key):
    seqs, half_len, cols = query.shape
    blk = half_len // 2
    heads = cols // HD
    return pl.pallas_call(
        _forward_kernel,
        grid=(seqs, 2),
        in_specs=[
            pl.BlockSpec((1, blk, cols), lambda s, q: (s, q, 0)),
            pl.BlockSpec((1, half_len, 2 * cols), lambda s, q: (s, 0, 0)),
            pl.BlockSpec((1, half_len, 2 * cols), lambda s, q: (s, 0, 0)),
            pl.BlockSpec((1, 1, blk), lambda s, q: (s, 0, q)),
            pl.BlockSpec((1, 2 * half_len, 1), lambda s, q: (s, 0, 0)),
        ],
        out_specs=[
            pl.BlockSpec((1, blk, cols), lambda s, q: (s, q, 0)),
            pl.BlockSpec((1, heads, blk), lambda s, q: (s, 0, q)),
        ],
        out_shape=[
            jax.ShapeDtypeStruct((seqs, half_len, cols), BF),
            jax.ShapeDtypeStruct((seqs, heads, half_len), F32),
        ],
        name="attend_forward",
    )(query, own, other, lab_query, lab_key)


def _backward_kernel(
    query_ref, own_ref, other_ref, lab_query_ref, lab_key_ref, grad_ref, log_ref,
    grad_query_ref, grad_own_ref, grad_other_ref, sums_ref, key_acc, value_acc,
):
    cols = query_ref.shape[2]
    half_len = own_ref.shape[1]
    heads = cols // HD
    first = pl.program_id(1) == 0
    same_doc = lab_key_ref[0] == lab_query_ref[0]
    pair = jnp.concatenate([own_ref[0], other_ref[0]], 0)
    grads = []
    key_parts = []
    value_parts = []
    for h in range(heads):
        at = slice(h * HD, (h + 1) * HD)
        query = query_ref[0][:, at]
        key = pair[:, at]
        value = pair[:, cols + h * HD : cols + (h + 1) * HD]
        grad_out = grad_ref[0][:, at]
        probs = jnp.exp(_scores(query, key, same_doc) - log_ref[0, h : h + 1, :])
        grad_probs = dot(value, grad_out, 1, 1)
        inner = jnp.sum(probs * grad_probs, axis=0, keepdims=True)
        grad_scores = (probs * (grad_probs - inner)).astype(BF)
        value_parts.append(dot(probs.astype(BF), grad_out, 1, 0))
        key_parts.append(dot(grad_scores, query, 1, 0) * SCALE)
        grads.append(dot(key, grad_scores, 0, 0) * SCALE)
    grad_query = jnp.concatenate(grads, 0).T
    grad_query_ref[0] = grad_query.astype(BF)
    key_part = jnp.concatenate(key_parts, 1)
    value_part = jnp.concatenate(value_parts, 1)
    sums = jnp.concatenate(
        [
            jnp.sum(grad_query, axis=0, keepdims=True),
            jnp.sum(value_part, axis=0, keepdims=True),
        ],
        0,
    )

    @pl.when(first)
    def _():
        key_acc[...] = key_part
        value_acc[...] = value_part
        sums_ref[0] = sums

    @pl.when(jnp.logical_not(first))
    def _():
        key_all = key_acc[...] + key_part
        value_all = value_acc[...] + value_part
        both = jnp.concatenate([key_all, value_all], 1).astype(BF)
        grad_own_ref[0] = both[:half_len]
        grad_other_ref[0] = both[half_len:]
        sums_ref[0] = sums_ref[0] + sums


def attend_backward(query, own, other, lab_query, lab_key, grad_heads, logs):
    seqs, half_len, cols = query.shape
    blk = half_len // 2
    heads = cols // HD
    return pl.pallas_call(
        _backward_kernel,
        grid=(seqs, 2),
        in_specs=[
            pl.BlockSpec((1, blk, cols), lambda s, q: (s, q, 0)),
            pl.BlockSpec((1, half_len, 2 * cols), lambda s, q: (s, 0, 0)),
            pl.BlockSpec((1, half_len, 2 * cols), lambda s, q: (s, 0, 0)),
            pl.BlockSpec((1, 1, blk), lambda s, q: (s, 0, q)),
            pl.BlockSpec((1, 2 * half_len, 1), lambda s, q: (s, 0, 0)),
            pl.BlockSpec((1, blk, cols), lambda s, q: (s, q, 0)),
            pl.BlockSpec((1, heads, blk), lambda s, q: (s, 0, q)),
        ],
        out_specs=[
            pl.BlockSpec((1, blk, cols), lambda s, q: (s, q, 0)),
            pl.BlockSpec((1, half_len, 2 * cols), lambda s, q: (s, 0, 0)),
            pl.BlockSpec((1, half_len, 2 * cols), lambda s, q: (s, 0, 0)),
            pl.BlockSpec((1, 2, cols), lambda s, q: (s, 0, 0)),
        ],
        out_shape=[
            jax.ShapeDtypeStruct((seqs, half_len, cols), BF),
            jax.ShapeDtypeStruct((seqs, half_len, 2 * cols), BF),
            jax.ShapeDtypeStruct((seqs, half_len, 2 * cols), BF),
            jax.ShapeDtypeStruct((seqs, 2, cols), F32),
        ],
        scratch_shapes=[
            pltpu.VMEM((2 * half_len, cols), F32),
            pltpu.VMEM((2 * half_len, cols), F32),
        ],
        name="attend_backward",
    )(query, own, other, lab_query, lab_key, grad_heads, logs)


def shards(
    tokens,
    time_embed,
    segments,
    w_qkv,
    w_out,
    w_up,
    w_down,
    qv_bias,
    up_bias,
    norm_gains,
    norm_shifts,
    branch_bias,
    out_grad,
):
    seqs, half_len, width = tokens.shape
    parts = lax.axis_size("tp")
    deep = lax.axis_size("shard")
    core = lax.axis_index("ctx")
    place = lax.axis_index("tp")
    rows = seqs * half_len
    blk = half_len // parts
    own_rows = seqs * blk
    cols = w_qkv.shape[2]
    units = w_up.shape[1]
    half_units = units // 2
    depth = w_qkv.shape[0]
    half_depth = depth // 2
    half_cols = cols // 2

    w_kvq = jnp.concatenate([w_qkv[:, 1], w_qkv[:, 2], w_qkv[:, 0]], 1)
    kvq_half = lax.dynamic_slice_in_dim(w_kvq, core * half_depth, half_depth, 0)
    out_half = lax.dynamic_slice_in_dim(w_out, core * half_cols, half_cols, 0)
    if half_cols == half_depth:
        front_own = gather_ordered(jnp.concatenate([kvq_half, out_half], 1), "shard")
        kvq_own, out_gathered = front_own[:, :, : 3 * cols], front_own[:, :, 3 * cols :]
    else:
        front_own = kvq_own = gather_ordered(kvq_half, "shard")
        out_gathered = gather_ordered(out_half, "shard")
    kvq_other = swap(kvq_own, "ctx", 1)
    full_kvq = in_order(kvq_own, kvq_other, core, 1).reshape(width, 3 * cols)

    up_half = lax.dynamic_slice_in_dim(w_up, core * half_units, half_units, 1)
    down_half = lax.dynamic_slice_in_dim(w_down, core * half_units, half_units, 0).T
    batch = jnp.concatenate([up_half, down_half], 1)
    batch, _ = lax.optimization_barrier((batch, front_own))
    if deep <= 4:
        near_list = gather_list(batch, "shard")
        far_list = [swap(piece, "tp", 2) for piece in near_list[:2]]
    bias_halves = up_bias.reshape(2, half_units)
    bias_near = jnp.where(core == 0, bias_halves, bias_halves[::-1])
    bias_far = swap(bias_near, "tp", 2)
    bias_pair = jnp.stack([bias_near, bias_far], 1).reshape(2 * units)

    stream_in = tokens.astype(F32) + time_embed[:, None, :]
    stream_low = stream_in.astype(BF).reshape(rows, width)
    kv_bias = jnp.concatenate([jnp.zeros_like(qv_bias[1]), qv_bias[1]])
    pair_own = (dot(stream_low, full_kvq[:, : 2 * cols], 1, 0) + kv_bias).astype(BF)
    pair_own = pair_own.reshape(seqs, half_len, 2 * cols)
    pair_other = swap(pair_own, "ctx", 1)
    query = (dot(stream_low, full_kvq[:, 2 * cols :], 1, 0) + qv_bias[0]).astype(BF)
    query = query.reshape(seqs, half_len, cols)
    labels_own = lax.dynamic_slice_in_dim(segments, core * half_len, half_len, 1)
    labels_other = lax.dynamic_slice_in_dim(segments, (1 - core) * half_len, half_len, 1)
    lab_query = labels_own[:, None, :]
    lab_key = jnp.concatenate([labels_own, labels_other], 1)[:, :, None]
    heads_low, logs = attend_forward(query, pair_own, pair_other, lab_query, lab_key)

    if deep <= 4:
        *held, _ = lax.optimization_barrier((*near_list, *far_list, heads_low))
        near_list, far_list = held[:deep], held[deep:]
        far_list = far_list + [swap(piece, "tp", 2) for piece in near_list[2:]]
        ffn_near = arrange(near_list, "shard").reshape(width, 2 * half_units)
        ffn_far = arrange(far_list, "shard").reshape(width, 2 * half_units)
    else:
        ffn_near = gather_ordered(batch, "shard").reshape(width, 2 * half_units)
        ffn_far = swap(ffn_near, "tp", 2)
    near_other = swap(ffn_near, "ctx", 1)
    far_other = swap(ffn_far, "ctx", 1)
    ffn_parts = (ffn_near, ffn_far, near_other, far_other)
    full_up = jnp.concatenate([part[:, :half_units] for part in ffn_parts], 1)
    full_down = jnp.concatenate([part[:, half_units:] for part in ffn_parts], 1)

    out_rows = jnp.transpose(out_gathered, (1, 0, 2)).reshape(half_cols, width)
    out_own = jnp.stack(gather_list(out_rows, "tp"))
    out_other = swap(out_own, "ctx", 1)
    full_out = in_order(out_own, out_other, core, 1).reshape(parts * cols, width)

    def block_of(values, m):
        return lax.dynamic_slice_in_dim(values, (place ^ m) * blk, blk, 1)

    heads_sent = [
        jnp.stack([block_of(heads_low, m), block_of(heads_low, m ^ 1)]) for m in range(parts)
    ]
    heads_parts = [heads_sent[0]] + [swap(heads_sent[m], "tp", m) for m in range(1, parts)]
    heads_parts = [part.reshape(2, own_rows, cols) for part in heads_parts]

    def feed_forward(side):
        stream = (block_of(tokens, side).astype(F32) + time_embed[:, None, :]).reshape(
            own_rows, width
        )
        heads_all = jnp.concatenate([part[side] for part in heads_parts], 1)
        attn_out = dot(heads_all, full_out, 1, 0) + branch_bias[0]
        scaled, scale = norm_stats(stream + attn_out)
        normed = scaled * norm_gains[0] + norm_shifts[0]
        normed_low = normed.astype(BF)
        pre_act = dot(normed_low, full_up, 1, 0) + bias_pair
        phi = 0.5 * (1.0 + lax.erf(pre_act * math.sqrt(0.5)))
        act_low = (pre_act * phi).astype(BF)
        slope = phi + pre_act * (
            jnp.exp(-0.5 * pre_act * pre_act) * (1.0 / math.sqrt(2.0 * math.pi))
        )
        return heads_all, scaled, scale, normed, normed_low, act_low, slope.astype(BF)

    def feed_backward(side, second_in, slope):
        cotangent = block_of(out_grad, side).astype(F32).reshape(own_rows, width)
        scaled, scale = norm_stats(second_in)
        grad_second = norm_grad(scaled, scale, cotangent, norm_gains[1])
        grad_ffn_low = grad_second.astype(BF)
        grad_pre = dot(grad_ffn_low, full_down, 1, 0) * slope.astype(F32)
        grad_pre_low = grad_pre.astype(BF)
        up_part = dot(grad_pre_low, full_up, 1, 1)
        return cotangent, scaled, grad_second, grad_ffn_low, grad_pre, grad_pre_low, up_part

    mate = feed_forward(1)
    down_mate = dot(mate[5], full_down, 1, 1).astype(BF)
    down_other = swap(down_mate, "tp", 1)
    own = feed_forward(0)
    heads_all, scaled_first, scale_first, normed, normed_low, act_low, slope = own
    down_part = dot(act_low, full_down, 1, 1)
    second_in = low(normed + down_part + down_other.astype(F32) + branch_bias[1])
    second_mate = swap(second_in, "tp", 1)
    (
        cotangent, scaled_second, grad_second, grad_ffn_low, grad_pre, grad_pre_low, up_part,
    ) = feed_backward(0, second_in.astype(F32), slope)
    (
        _, _, _, grad_ffn_mate, grad_pre_mate, grad_pre_low_mate, up_part_mate,
    ) = feed_backward(1, second_mate.astype(F32), mate[6])
    up_other = swap(up_part_mate.astype(BF), "tp", 1)
    scaled_both, _ = norm_stats(jnp.concatenate([second_in, second_mate]).astype(F32))
    layer_rows = low(scaled_both * norm_gains[1] + norm_shifts[1]).reshape(2, own_rows, width)
    layer_far = swap(layer_rows, "tp", 2)

    both_normed = jnp.concatenate([normed_low, mate[4]])
    both_pre = jnp.concatenate([grad_pre_low, grad_pre_low_mate])
    both_grad = jnp.concatenate([grad_ffn_low, grad_ffn_mate])
    both_act = jnp.concatenate([act_low, mate[5]])
    up_sent = dot(both_normed, both_pre[:, units:], 0, 0).astype(BF)
    down_sent = dot(both_grad, both_act[:, units:], 0, 0).astype(BF)
    up_got = swap(up_sent, "ctx", 1)
    down_got = swap(down_sent, "ctx", 1)
    up_sum = dot(both_normed, both_pre[:, :units], 0, 0) + up_got.astype(F32)
    down_sum = dot(both_grad, both_act[:, :units], 0, 0) + down_got.astype(F32)
    far_sum = jnp.concatenate([up_sum[:, half_units:], down_sum[:, half_units:]], 1).astype(BF)
    far_got = swap(far_sum, "tp", 2)

    grad_normed = up_part + up_other.astype(F32) + grad_second
    grad_first = norm_grad(scaled_first, scale_first, grad_normed, norm_gains[0])
    grad_attn_low = grad_first.astype(BF)
    grad_heads_own = dot(grad_attn_low, full_out, 1, 1).astype(BF)
    grad_parts = [grad_heads_own[:, m * cols : (m + 1) * cols] for m in range(parts)]
    grad_parts = [grad_parts[0]] + [swap(grad_parts[m], "tp", m) for m in range(1, parts)]
    grad_heads = jnp.zeros((seqs, parts, blk, cols), BF)
    for m in range(parts):
        grad_heads = lax.dynamic_update_index_in_dim(
            grad_heads, grad_parts[m].reshape(seqs, blk, cols), place ^ m, 1
        )
    grad_heads = grad_heads.reshape(seqs, half_len, cols)
    grad_heads, _ = lax.optimization_barrier((grad_heads, far_sum))
    grad_query, grad_pair_own, grad_pair_other, sums = attend_backward(
        query, pair_own, pair_other, lab_query, lab_key, grad_heads, logs
    )
    grad_pair = (grad_pair_own.astype(F32) + swap(grad_pair_other, "ctx", 1).astype(F32)).astype(BF)
    grad_prod_low = jnp.concatenate([grad_pair, grad_query], 2).reshape(rows, 3 * cols)
    qkv_part = dot(grad_prod_low, full_kvq, 1, 1).astype(BF).reshape(seqs, parts, blk, width)
    input_own = grad_first.reshape(seqs, blk, width) + lax.dynamic_index_in_dim(
        qkv_part, place, 1, False
    ).astype(F32)
    for m in range(1, parts):
        sent = lax.dynamic_index_in_dim(qkv_part, place ^ m, 1, False)
        input_own = input_own + swap(sent, "tp", m).astype(F32)
    near_sum = jnp.concatenate([up_sum[:, :half_units], down_sum[:, :half_units]], 1)
    ffn_sum = (near_sum + far_got.astype(F32)).astype(BF)
    input_low, _ = lax.optimization_barrier((low(input_own), ffn_sum))
    input_list = gather_list(input_low, "tp")

    def lay_out(blocks):
        out = jnp.zeros((seqs, parts, blk, width), F32)
        for m, block in enumerate(blocks):
            out = lax.dynamic_update_index_in_dim(
                out, block.astype(F32).reshape(seqs, blk, width), place ^ m, 1
            )
        return out.reshape(seqs, half_len, width)

    input_grad = lay_out(input_list)
    layer_out = lay_out([layer_rows[0], layer_rows[1], layer_far[0], layer_far[1]])

    ffn_sum = reduce_chunks(ffn_sum.reshape(deep, depth, 2 * half_units), "shard")
    ffn_sum = low(ffn_sum)
    ffn_both = in_order(
        ffn_sum.reshape(depth, 2, half_units),
        swap(ffn_sum, "ctx", 1).reshape(depth, 2, half_units),
        core,
        2,
    ).astype(F32)
    up_share = ffn_both[:, 0]
    down_share = ffn_both[:, 1].T

    grad_out = dot(heads_all, grad_attn_low, 0, 0).astype(BF).reshape(parts, 2, half_cols, width)
    out_sum = lax.dynamic_index_in_dim(grad_out, core, 1, False).astype(F32) + swap(
        lax.dynamic_index_in_dim(grad_out, 1 - core, 1, False), "ctx", 1
    ).astype(F32)
    out_low = out_sum.astype(BF)
    out_sum = out_sum[0]
    for m in range(1, parts):
        out_sum = out_sum + swap(out_low[m], "tp", m).astype(F32)
    out_chunks = jnp.transpose(out_sum.reshape(half_cols, deep, depth), (1, 0, 2)).astype(BF)
    grad_qkv = dot(stream_low, grad_prod_low, 0, 0).astype(BF)
    grad_qkv = grad_qkv.reshape(deep, 2, half_depth, 3 * cols)
    qkv_sum = lax.dynamic_index_in_dim(grad_qkv, core, 1, False).astype(F32) + swap(
        lax.dynamic_index_in_dim(grad_qkv, 1 - core, 1, False), "ctx", 1
    ).astype(F32)
    if half_cols == half_depth:
        front_sum = reduce_chunks(jnp.concatenate([qkv_sum.astype(BF), out_chunks], 2), "shard")
        front_sum = low(front_sum)
        front_both = in_order(front_sum, swap(front_sum, "ctx", 1), core, 0).astype(F32)
        kvq_share, out_share = front_both[:, : 3 * cols], front_both[:, 3 * cols :]
    else:
        qkv_sum = reduce_chunks(qkv_sum.astype(BF), "shard")
        out_sum = reduce_chunks(out_chunks, "shard")
        kvq_share = in_order(qkv_sum, swap(qkv_sum, "ctx", 1), core, 0)
        out_share = in_order(out_sum, swap(out_sum, "ctx", 1), core, 0)
    kvq_share = kvq_share.reshape(depth, 3, cols)
    qkv_share = jnp.stack([kvq_share[:, 2], kvq_share[:, 0], kvq_share[:, 1]], 1)

    norm_terms = jnp.concatenate(
        [
            jnp.sum(grad_normed * scaled_first, axis=0),
            jnp.sum(cotangent * scaled_second, axis=0),
            jnp.sum(grad_normed, axis=0),
            jnp.sum(cotangent, axis=0),
            jnp.sum(grad_first, axis=0),
            jnp.sum(grad_second, axis=0),
        ]
    )
    up_rel = (jnp.sum(grad_pre, axis=0) + jnp.sum(grad_pre_mate, axis=0)).reshape(
        2, 2, half_units
    )
    up_terms = in_order(up_rel[0], up_rel[1], core, 1)
    norm_terms, up_own, up_far, _ = lax.optimization_barrier(
        (norm_terms, up_terms[0], up_terms[1], qkv_part)
    )
    got = swap(jnp.concatenate([norm_terms, up_far]), "tp", 2)
    norm_terms = norm_terms + got[: 6 * width]
    norm_terms = norm_terms + swap(norm_terms, "tp", 1)
    small = jnp.concatenate(
        [norm_terms, up_own + got[6 * width :], jnp.sum(sums, axis=0).reshape(2 * cols)]
    )
    small = small + swap(small, "ctx", 1)
    step = 1
    while step < deep:
        small = small + swap(small, "shard", step)
        step *= 2
    norm_sum = small[: 6 * width].reshape(3, 2, width)
    up_total = small[6 * width : 6 * width + units]
    qv_sum = small[6 * width + units :].reshape(2, cols)
    return (
        layer_out,
        input_grad,
        qkv_share,
        out_share,
        up_share,
        down_share,
        qv_sum,
        up_total,
        norm_sum[0],
        norm_sum[1],
        norm_sum[2],
    )


def solution(mesh):
    placed = (
        P("shard", "ctx", None),
        P("shard", None),
        P("shard", None),
        P("shard", None, "tp"),
        P("tp", "shard"),
        P("shard", "tp"),
        P("tp", "shard"),
        P(None, "tp"),
        P("tp"),
        P(),
        P(),
        P(),
        P("shard", "ctx", None),
    )

    return jax.shard_map(
        shards,
        mesh=mesh,
        in_specs=placed,
        out_specs=(
            P("shard", "ctx", None),
            P("shard", "ctx", None),
            P("shard", None, "tp"),
            P("tp", "shard"),
            P("shard", "tp"),
            P("tp", "shard"),
            P(None, "tp"),
            P("tp"),
            P(),
            P(),
            P(),
        ),
        check_vma=False,
    )
```
